256 devices in a mesh: pair: 128 (over y_lo, z, x, core), trow: 2 (over y_hi).
Axes of the slice: x: 4, y: 4 (y_hi: 2, y_lo: 2; y = y_hi * 2 + y_lo), z: 8, core: 2. Of those that a mesh axis runs over, the one named last changes fastest.
Arguments:
- query_bank: bfloat16 [128, 64, 1024], P('pair'), may hold values from -6 to 6
- ref_owner: int32 [1], replicated, may hold values from 0 to 127
- target_feat: bfloat16 [128, 512, 1024], P('pair', None, 'trow'), may hold values from -60 to 60
- valid_rows: int32 [128], P('pair'), may hold values from 2 to 16, as said below
- w_first: bfloat16 [16, 1, 3, 3, 3, 3], replicated, may hold values from -2 to 2
- b_first: float32 [16], replicated, may hold values from -0.5 to 0.5
- w_middle: bfloat16 [16, 16, 3, 3, 3, 3], replicated, may hold values from -0.25 to 0.25
- b_middle: float32 [16], replicated, may hold values from -0.5 to 0.5
- w_last: bfloat16 [1, 16, 3, 3, 3, 3], replicated, may hold values from -0.25 to 0.25
- b_last: float32 [1], replicated, may hold values from -0.5 to 0.5
Outputs:
- scores: float32 [128, 64, 512], P('pair', None, 'trow')
The draws below stay inside these ranges and needn't reach their ends.
Inputs may be any that keep to these rules, and one draw needn't show every extreme that they name: ref_owner names the group along pair whose window is the reference. Rows of a target grid at or past valid_rows are padding; some pair fills all 16 rows.
All inputs are finite; a program needn't handle non-finite values.
Results may differ from the reference program's by a relative error of at most 0.007.
Values may be sent and summed in bfloat16 or wider, within the bound.
A program may use at most 64 MiB of HBM per device.

```python
import math
import jax
import jax.numpy as jnp
from jax import lax

C = 1024
CH = 16
HB = 16
WB = 32
WA = 32
GROUPS = 128
PAIRS = 128
NA = 64
NB = 512


def draw_target_feat(key, part):
    key_base = jax.random.fold_in(key, 11)
    key_scale = jax.random.fold_in(key, 12)
    row_scale = jnp.exp(jax.random.uniform(key_scale, (PAIRS, NB, 1), jnp.float32, 0.0, math.log(10.0)))
    samples = jax.random.normal(key_base, (PAIRS, NB, C), jnp.float32) * row_scale
    return jnp.clip(samples, -60.0, 60.0).astype(jnp.bfloat16)


def draw_valid_rows(key, part):
    key_rows = jax.random.fold_in(key, 21)
    key_spot = jax.random.fold_in(key, 22)
    counts = jax.random.randint(key_rows, (PAIRS,), 2, HB + 1)
    chosen = jax.random.randint(key_spot, (2,), 0, PAIRS)
    position = jnp.arange(PAIRS)
    counts = jnp.where(position == chosen[0], HB, counts)
    counts = jnp.where((position == chosen[1]) & (chosen[1] != chosen[0]), 2, counts)
    return counts.astype(jnp.int32)


def levels(stream_key, shape, split, smallest, high):
    level, own = 1.0, jax.random.fold_in(stream_key, 6)
    for dim, blocks in split:
        steps = jnp.exp(jax.random.uniform(jax.random.fold_in(own, dim), (blocks,), jnp.float32, smallest / len(split), high / len(split)))
        level = level * jnp.repeat(steps, shape[dim] // blocks).reshape([-1 if axis == dim else 1 for axis in range(len(shape))])
    return level


def scatter_about(stream_key, dims, scale, most, pieces=(), kind=jnp.bfloat16):
    level = levels(stream_key, dims, pieces, -0.22, 0.18) if pieces else 1.0
    entries = jax.random.normal(stream_key, dims, jnp.float32) * scale * level
    return jnp.minimum(jnp.maximum(entries, -most), most).astype(kind)


def setup_inputs(seed: int = 0) -> dict:
    splits = jax.random.split(jax.random.key(seed), 11)
    query_bank = scatter_about(splits[0], (GROUPS, NA, C), 1.0, 6.0, ((0, 128),))
    ref_owner = jax.random.randint(splits[1], (1,), 0, GROUPS).astype(jnp.int32)
    target_feat = draw_target_feat(jax.random.fold_in(splits[10], 71), 0)
    valid_rows = draw_valid_rows(jax.random.fold_in(splits[10], 71), 0)
    w_first = scatter_about(splits[4], (CH, 1, 3, 3, 3, 3), 9 ** -0.5, 2.0)
    b_first = jnp.clip(jax.random.uniform(splits[5], (CH,), jnp.float32, -0.5, 0.5), -0.5, 0.5)
    w_middle = scatter_about(splits[6], (CH, CH, 3, 3, 3, 3), (81 * CH // 2) ** -0.5, 0.25)
    b_middle = jnp.clip(jax.random.uniform(splits[7], (CH,), jnp.float32, -0.5, 0.5), -0.5, 0.5)
    w_last = scatter_about(splits[8], (1, CH, 3, 3, 3, 3), (81 * CH // 2) ** -0.5, 0.25)
    b_last = jnp.clip(jax.random.uniform(splits[9], (1,), jnp.float32, -0.5, 0.5), -0.5, 0.5)
    return dict(query_bank=query_bank, ref_owner=ref_owner, target_feat=target_feat, valid_rows=valid_rows, w_first=w_first, b_first=b_first, w_middle=w_middle, b_middle=b_middle, w_last=w_last, b_last=b_last)


EPS_NORM = 1e-06
EPS_PEAK = 1e-05

def shift_along(values, offset, axis_dim):
    if offset == 0:
        return values
    length = values.shape[axis_dim]
    zero_shape = list(values.shape)
    zero_shape[axis_dim] = abs(offset)
    zero_block = jnp.zeros(zero_shape, values.dtype)
    if offset > 0:
        return jnp.concatenate([lax.slice_in_dim(values, offset, length, axis=axis_dim), zero_block], axis=axis_dim)
    return jnp.concatenate([zero_block, lax.slice_in_dim(values, 0, length + offset, axis=axis_dim)], axis=axis_dim)

def block_conv(row_block, weight_matrix, out_channels, block_rows, exact):
    extent = row_block.shape[2]
    column_pos = jnp.arange(extent, dtype=jnp.int32) % WB
    shifted = []
    for col_off in (-1, 0, 1):
        in_range = (column_pos + col_off >= 0) & (column_pos + col_off < WB)
        moved_cols = shift_along(row_block, col_off, 2)
        shifted.append(jnp.where(in_range[None, None, :], moved_cols, jnp.zeros((), row_block.dtype)))
    layers = []
    for row_off in range(3):
        for col_idx in range(3):
            layers.append(lax.slice_in_dim(shifted[col_idx], row_off * WB, (row_off + block_rows) * WB, axis=2))
    stacked = jnp.concatenate(layers, axis=0)
    if exact:
        products = jnp.einsum('pk,kab->pab', weight_matrix.astype(jnp.float32), stacked.astype(jnp.float32))
    else:
        products = jnp.einsum('pk,kab->pab', weight_matrix, stacked, preferred_element_type=jnp.float32)
    positions = row_block.shape[1]
    query_row = jnp.arange(positions, dtype=jnp.int32) // WA
    query_col = jnp.arange(positions, dtype=jnp.int32) % WA
    ref_rows = positions // WA
    accumulated = jnp.zeros((out_channels, positions, block_rows * WB), jnp.float32)
    for row_off in range(3):
        for col_off in range(3):
            start_chan = (row_off * 3 + col_off) * out_channels
            offset_group = products[start_chan:start_chan + out_channels]
            in_range = (query_row + row_off - 1 >= 0) & (query_row + row_off - 1 < ref_rows)
            in_range = in_range & (query_col + col_off - 1 >= 0) & (query_col + col_off - 1 < WA)
            moved_group = shift_along(offset_group, (row_off - 1) * WA + col_off - 1, 1)
            accumulated = accumulated + jnp.where(in_range[None, :, None], moved_group, 0.0)
    return accumulated

def conv_layer(inputs, weight, bias, exact):
    out_channels = weight.shape[0]
    in_channels = weight.shape[1]
    weight_matrix = jnp.transpose(weight, (2, 3, 0, 4, 5, 1)).reshape(9 * out_channels, 9 * in_channels)
    rows_out = inputs.shape[2] // WB - 2
    block_rows = 1
    for option in (2, 4):
        if rows_out % option == 0:
            block_rows = option

    def one_block(block_index):
        row_block = lax.dynamic_slice_in_dim(inputs, block_index * (block_rows * WB), (block_rows + 2) * WB, 2)
        return block_conv(row_block, weight_matrix, out_channels, block_rows, exact)
    block_outputs = lax.map(one_block, jnp.arange(rows_out // block_rows, dtype=jnp.int32))
    joined = jnp.transpose(block_outputs, (1, 2, 0, 3)).reshape(out_channels, inputs.shape[1], rows_out * WB)
    return joined + bias[:, None, None]

def unit_rows(features):
    values = features.astype(jnp.float32)
    return (values * lax.rsqrt(lax.optimization_barrier(jnp.sum(values * values, axis=1, keepdims=True)) + EPS_NORM)).astype(jnp.bfloat16)

def contract(left, right):
    return lax.dot_general(left, right, (((1,), (1,)), ((), ())), preferred_element_type=jnp.float32)

def reference(query_bank, ref_owner, target_feat, valid_rows, w_first, b_first, w_middle, b_middle, w_last, b_last):
    query_vec = lax.dynamic_index_in_dim(query_bank, ref_owner[0], 0, keepdims=False)
    unit_query = unit_rows(query_vec)
    cos_scale = math.sqrt(query_bank.shape[2])
    global_row = jnp.arange(HB * WB, dtype=jnp.int32) // WB

    def one_pair(pair_item):
        target, row_count = pair_item
        raw_dot = contract(unit_query, target)
        squares = lax.optimization_barrier(jnp.sum(jnp.square(target.astype(jnp.float32)), axis=1))
        is_live = global_row < row_count
        correlation = jnp.where(is_live[None, :], cos_scale * raw_dot * lax.rsqrt(squares + EPS_NORM)[None, :], 0.0)
        magnitude = jnp.abs(correlation)
        peak_query = lax.optimization_barrier(jnp.max(magnitude, axis=0))
        peak_target = lax.optimization_barrier(jnp.max(magnitude, axis=1))
        volume = correlation * (correlation / (peak_query[None, :] + EPS_PEAK)) * (correlation / (peak_target[:, None] + EPS_PEAK))
        volume = volume.astype(jnp.bfloat16)[None]
        padded = jnp.pad(volume, ((0, 0), (0, 0), (WB, WB)))
        hidden = jnp.maximum(conv_layer(padded, w_first, b_first, True), 0.0).astype(jnp.bfloat16)
        padded = jnp.pad(hidden, ((0, 0), (0, 0), (WB, WB)))
        hidden = jnp.maximum(conv_layer(padded, w_middle, b_middle, True), 0.0).astype(jnp.bfloat16)
        padded = jnp.pad(hidden, ((0, 0), (0, 0), (WB, WB)))
        result = conv_layer(padded, w_last, b_last, True)[0]
        return jnp.where(is_live[None, :], result, 0.0)
    return lax.map(one_pair, (target_feat, valid_rows))
```

```python
import functools
import math

import jax
import jax.numpy as jnp
from jax import lax
from jax.experimental import pallas as pl
from jax.experimental.pallas import tpu as pltpu
from jax.sharding import PartitionSpec as P

MESH = pl.DeviceIdType.MESH
WB = 32
WA = 32
HB = 16
NB = HB * WB
NA = 64
EPS_NORM = 1e-06
EPS_PEAK = 1e-05
F32 = jnp.float32
BF16 = jnp.bfloat16

BLOCKS = 6
STEP = 6
SLOTS = 32


def nt(left, right):
    return lax.dot_general(left, right, (((1,), (1,)), ((), ())), preferred_element_type=F32)


def nn(left, right):
    return lax.dot_general(left, right, (((1,), (0,)), ((), ())), preferred_element_type=F32)


def iota(shape, dim):
    return lax.broadcasted_iota(jnp.int32, shape, dim)


def comm_kernel(n, places, owner_ref, q_ref, tf_ref, u_ref, other_ref, unit, recv, pick, gath, sems, feat_sems):
    per = SLOTS // places
    stride = n // places
    me = lax.axis_index("pair")
    plane = lax.axis_index("trow")
    is_place = lax.rem(me, stride) == 0
    my_place = me // stride

    barrier = pltpu.get_barrier_semaphore()

    def greet(pair, trow):
        @pl.when(jnp.logical_or(pair != me, trow != plane))
        def _():
            pl.semaphore_signal(barrier, inc=1, device_id=(pair, trow), device_id_type=MESH)

    @pl.loop(0, places)
    def _(p):
        greet(p * stride, plane)
        greet(p * stride, 1 - plane)

    greet(me, 1 - plane)

    @pl.when(is_place)
    def _():
        @pl.loop(0, n)
        def _(d):
            greet(d, plane)

    values = q_ref[0].astype(F32)
    scale = lax.rsqrt(jnp.sum(values * values, axis=1, keepdims=True) + EPS_NORM)
    normed = values * scale
    for half in range(2):
        for s in range(SLOTS):
            g, t = s // 4, s % 4
            piece = normed[8 * g : 8 * g + 8, 512 * half + 128 * t : 512 * half + 128 * t + 128]
            unit[half, s // per, 8 * (s % per) : 8 * (s % per) + 8, :] = piece.astype(BF16)

    @pl.when(is_place)
    def _():
        pl.semaphore_wait(barrier, (2 * n - 1) + (places - 1) + 1)

    @pl.when(jnp.logical_not(is_place))
    def _():
        pl.semaphore_wait(barrier, places + 1)

    features = pltpu.make_async_remote_copy(
        src_ref=tf_ref.at[0],
        dst_ref=other_ref,
        send_sem=feat_sems.at[0],
        recv_sem=feat_sems.at[1],
        device_id=(me, 1 - plane),
        device_id_type=MESH,
    )
    features.start()

    @pl.loop(0, places)
    def _(p):
        @pl.when(p * stride != me)
        def _():
            pltpu.make_async_remote_copy(
                src_ref=unit.at[plane, p],
                dst_ref=recv.at[me],
                send_sem=sems.at[0],
                recv_sem=sems.at[1],
                device_id=(p * stride, plane),
                device_id_type=MESH,
            ).start()

    @pl.when(is_place)
    def _():
        own = pltpu.make_async_copy(unit.at[plane, my_place], recv.at[me], sems.at[4])
        own.start()
        own.wait()
        rest = recv.at[pl.ds(0, n - 1)]
        pltpu.make_async_copy(rest, rest, sems.at[1]).wait()
        chosen = recv[owner_ref[0]]
        pick[...] = chosen
        gath[plane * places + my_place] = chosen

        @pl.loop(1, n)
        def _(o):
            pltpu.make_async_remote_copy(
                src_ref=pick,
                dst_ref=gath.at[plane * places + my_place],
                send_sem=sems.at[2],
                recv_sem=sems.at[3],
                device_id=(lax.rem(me + o, n), plane),
                device_id_type=MESH,
            ).start()

        @pl.loop(0, n)
        def _(o):
            pltpu.make_async_remote_copy(
                src_ref=pick,
                dst_ref=gath.at[plane * places + my_place],
                send_sem=sems.at[5],
                recv_sem=sems.at[3],
                device_id=(lax.rem(me + o, n), 1 - plane),
                device_id_type=MESH,
            ).start()

        part = gath.at[pl.ds(0, 2 * places - 1)]
        pltpu.make_async_copy(part, part, sems.at[3]).wait()
        part = recv.at[pl.ds(0, n - 1)]
        pltpu.make_async_copy(part, part, sems.at[2]).wait()
        pltpu.make_async_copy(recv, recv, sems.at[5]).wait()
        if places > 1:
            part = unit.at[0, pl.ds(0, places - 1)]
            pltpu.make_async_copy(part, part, sems.at[0]).wait()

    @pl.when(jnp.logical_not(is_place))
    def _():
        pltpu.make_async_copy(gath, gath, sems.at[3]).wait()
        part = unit.at[0]
        pltpu.make_async_copy(part, part, sems.at[0]).wait()

    for half in range(2):
        rows = []
        for g in range(8):
            tiles = []
            for t in range(4):
                s = 4 * g + t
                tiles.append(gath[half * places + s // per, 8 * (s % per) : 8 * (s % per) + 8, :].astype(F32))
            rows.append(jnp.concatenate(tiles, axis=1))
        u_ref[half] = jnp.concatenate(rows, axis=0).astype(BF16)

    features.wait()


def exchange(owner, bank, feats, n):
    places = min(SLOTS, n)
    per = SLOTS // places
    return pl.pallas_call(
        functools.partial(comm_kernel, n, places),
        out_shape=(
            jax.ShapeDtypeStruct((2, NA, 512), BF16),
            jax.ShapeDtypeStruct((NB, 512), BF16),
        ),
        in_specs=[
            pl.BlockSpec(memory_space=pltpu.SMEM),
            pl.BlockSpec(memory_space=pltpu.VMEM),
            pl.BlockSpec(memory_space=pl.ANY),
        ],
        out_specs=(
            pl.BlockSpec(memory_space=pltpu.VMEM),
            pl.BlockSpec(memory_space=pl.ANY),
        ),
        scratch_shapes=[
            pltpu.VMEM((2, places, per * 8, 128), BF16),
            pltpu.VMEM((n, per * 8, 128), BF16),
            pltpu.VMEM((per * 8, 128), BF16),
            pltpu.VMEM((2 * places, per * 8, 128), BF16),
            pltpu.SemaphoreType.DMA((6,)),
            pltpu.SemaphoreType.DMA((2,)),
        ],
        compiler_params=pltpu.CompilerParams(collective_id=0, has_side_effects=True),
        name="window_exchange",
    )(owner, bank, feats)


def spread_rows(src_ref, tmp):
    tmp[...] = jnp.zeros_like(tmp)
    for t in range(27):
        tmp[t, 0:3, 0:16] = src_ref[t].astype(F32)
    flat = tmp[...].reshape(216, 128).astype(BF16)
    take = (iota((128, 128), 1) % 16 == iota((128, 128), 0)).astype(F32).astype(BF16)
    return nn(flat, take)


def bias_row(b_ref, used):
    lane = iota((1, 256), 1)
    row = jnp.zeros((1, 256), F32)
    for o in range(16):
        row = jnp.where(lane % 16 == o, b_ref[o], row)
    return jnp.where(lane < used, row, 0.0)


def prepare(wf_ref, wm_ref, wl_ref, tmp, spread, w1, w2, w3):
    spread[0:216, :] = spread_rows(wf_ref, tmp)
    row = iota((32, 128), 0)
    lane = iota((32, 128), 1)
    for tile in range(2):
        j_of = row // 2 - (tile * 4 + lane // 32)
        i_of = row % 2 - (lane // 16) % 2 + 1
        for k in range(3):
            for l in range(4):
                block = jnp.zeros((32, 128), F32)
                if l < 3:
                    for i in range(3):
                        for j in range(3):
                            t = (i * 3 + j) * 3 + k
                            value = spread[8 * t + l : 8 * t + l + 1, :]
                            block = jnp.where((j_of == j) & (i_of == i), value, block)
                w1[k, 32 * l : 32 * l + 32, 128 * tile : 128 * tile + 128] = block.astype(BF16)

    spread[0:216, :] = spread_rows(wl_ref, tmp)
    w3[...] = jnp.zeros_like(w3)
    odd1 = (iota((1, 128), 1) // 16) % 2 == 1
    for half in range(2):
        for tile in range(12):
            m, first = tile // 2, (tile % 2) * 4
            columns = [6 * m + q for q in range(first, first + 4) if q < STEP and 6 * m + q < WA]
            if not columns or columns[-1] < 16 * half - 1 or columns[0] > 16 * half + 16:
                continue
            q_of = first + iota((16, 128), 1) // 32
            c_in = 6 * m + q_of
            j_of = c_in - (16 * half + iota((16, 128), 0)) + 1
            j_of = jnp.where((q_of < STEP) & (c_in < WA), j_of, -1)
            for k in range(3):
                for l in range(3):
                    for ra in range(2):
                        block = jnp.zeros((16, 128), F32)
                        for j in range(3):
                            t0 = ((1 - ra) * 3 + j) * 3 + k
                            t1 = ((2 - ra) * 3 + j) * 3 + k
                            value = jnp.where(
                                odd1,
                                spread[8 * t1 + l : 8 * t1 + l + 1, :],
                                spread[8 * t0 + l : 8 * t0 + l + 1, :],
                            )
                            block = jnp.where(j_of == j, value, block)
                        at = 64 * l + 32 * ra + 16 * half
                        w3[k, at : at + 16, 128 * tile : 128 * tile + 128] = block.astype(BF16)

    take = (iota((16, 128), 1) % 16 == iota((16, 128), 0)).astype(F32).astype(BF16)
    spread[...] = nn(wm_ref[...].reshape(81 * 16, 16), take)
    odd = (iota((16, 128), 1) // 16) % 2 == 1
    p_of = iota((16, 128), 1) // 32
    for k in range(3):
        for l in range(3):
            w2[3 * k + l, 192:256, :] = jnp.zeros((64, 256), BF16)
            for ra in range(2):
                values = []
                for j in range(3):
                    t0 = (((1 - ra) * 3 + j) * 3 + k) * 3 + l
                    t1 = (((2 - ra) * 3 + j) * 3 + k) * 3 + l
                    values.append(
                        jnp.where(odd, spread[16 * t1 : 16 * t1 + 16, :], spread[16 * t0 : 16 * t0 + 16, :])
                    )
                for q in range(STEP):
                    for tile in range(2):
                        block = jnp.zeros((16, 128), F32)
                        for j in range(3):
                            block = jnp.where(p_of == q + j - 4 * tile, values[j], block)
                        at = 32 * q + 16 * ra
                        w2[3 * k + l, at : at + 16, 128 * tile : 128 * tile + 128] = block.astype(BF16)


def shifted(values, by, edge):
    rows = values.shape[0]
    moved = pltpu.roll(values, by % rows, 0)
    return jnp.where(iota(values.shape, 0) % WB == edge, 0.0, moved)


def score_kernel(
    valid_ref, bf_ref, bm_ref, bl_ref, u_ref, own_ref, oth_ref, e_ref, wf_ref, wm_ref, wl_ref,
    out_ref, tmp, spread, w1, w2, w3, vbuf, xbuf, h1, h2,
):
    rank = lax.axis_index("trow")
    prepare(wf_ref, wm_ref, wl_ref, tmp, spread, w1, w2, w3)
    b1 = bias_row(bf_ref, 256)
    b2 = bias_row(bm_ref, 32 * STEP)

    own = own_ref[0]
    oth = oth_ref[...]
    u_own = u_ref[rank]
    u_oth = u_ref[1 - rank]
    raw = nt(own, jnp.concatenate([u_own] * 4, axis=0)) + nt(oth, jnp.concatenate([u_oth] * 4, axis=0))
    own32 = own.astype(F32)
    oth32 = oth.astype(F32)
    squares = jnp.sum(own32 * own32 + oth32 * oth32, axis=1, keepdims=True)
    live = iota((NB, 1), 0) // WB < valid_ref[0]
    corr = jnp.where(live, math.sqrt(1024) * raw * lax.rsqrt(squares + EPS_NORM), 0.0)
    magnitude = jnp.abs(corr)
    peak_query = jnp.max(magnitude, axis=1, keepdims=True)
    peak_target = jnp.max(magnitude, axis=0, keepdims=True)
    volume = corr * (corr * (1.0 / (peak_query + EPS_PEAK))) * (corr * (1.0 / (peak_target + EPS_PEAK)))
    lane = iota((NB, 256), 1)
    chosen = jnp.where(
        lane < 64, shifted(volume, 1, 0), jnp.where(lane < 128, volume, shifted(volume, -1, WB - 1))
    )
    vbuf[0:WB, :] = jnp.zeros((WB, 256), BF16)
    vbuf[WB + NB : 2 * WB + NB, :] = jnp.zeros((WB, 256), BF16)
    vbuf[WB : WB + NB, :] = chosen.astype(BF16)
    start = pl.multiple_of(rank * (6 * WB), 6 * WB)
    xbuf[...] = nn(vbuf[pl.ds(start, 12 * WB), :], e_ref[...]).astype(BF16)

    pad = pl.multiple_of((1 - rank) * WB, WB)

    lane = iota((10 * WB, 256), 1)
    for m in range(BLOCKS):
        acc = nn(xbuf[0 : 10 * WB, 128 * m : 128 * m + 128], w1[0])
        for k in (1, 2):
            acc = acc + nn(xbuf[WB * k : WB * k + 10 * WB, 128 * m : 128 * m + 128], w1[k])
        hidden = jnp.maximum(acc + b1, 0.0)
        if m == 0:
            hidden = jnp.where(lane < 32, 0.0, hidden)
        if m == BLOCKS - 1:
            hidden = jnp.where(lane >= 32 * (WA - 6 * m + 1), 0.0, hidden)
        zero = jnp.zeros((WB, 256), BF16)
        edge = pl.multiple_of(rank * (10 * WB), WB)
        for l in range(3):
            h1[m, l, pl.ds(edge, WB), :] = zero
        h1[m, 0, pl.ds(pad, 10 * WB), :] = shifted(hidden, 1, 0).astype(BF16)
        h1[m, 1, pl.ds(pad, 10 * WB), :] = hidden.astype(BF16)
        h1[m, 2, pl.ds(pad, 10 * WB), :] = shifted(hidden, -1, WB - 1).astype(BF16)

    edge = pl.multiple_of(rank * (9 * WB), WB)
    for m in range(BLOCKS):
        acc = jnp.zeros((9 * WB, 256), F32)
        for k in range(3):
            for l in range(3):
                acc = acc + nt(h1[m, l, WB * k : WB * k + 9 * WB, :], w2[3 * k + l])
        hidden = jnp.maximum(acc + b2, 0.0)
        h2[pl.ds(edge, WB), 256 * m : 256 * m + 256] = jnp.zeros((WB, 256), BF16)
        h2[pl.ds(pad, 9 * WB), 256 * m : 256 * m + 256] = hidden.astype(BF16)

    acc = nt(w3[0], h2[0 : 8 * WB, :])
    for k in (1, 2):
        acc = acc + nt(w3[k], h2[WB * k : WB * k + 8 * WB, :])
    column = iota((NA, 8 * WB), 1) % WB
    result = acc[NA : 2 * NA]
    result = result + jnp.where(column == 0, 0.0, pltpu.roll(acc[0:NA], 1, 1))
    result = result + jnp.where(column == WB - 1, 0.0, pltpu.roll(acc[2 * NA : 3 * NA], 8 * WB - 1, 1))
    result = result + bl_ref[0]
    row = rank * 8 + iota((NA, 8 * WB), 1) // WB
    out_ref[0] = jnp.where(row < valid_ref[0], result, 0.0)


def copy_matrix():
    source = jnp.arange(256, dtype=jnp.int32)[:, None]
    lane = jnp.arange(768, dtype=jnp.int32)[None, :]
    block, shift, inner = lane // 128, (lane // 32) % 4, lane % 32
    column, ref_row = 6 * block - 2 + inner // 2, inner % 2
    used = (inner < 20) & (column >= 0) & (column < WA) & (shift < 3)
    return (used & (source == shift * 64 + ref_row * WA + column)).astype(BF16)


def score(valid, b_first, b_middle, b_last, unit, own, other, wf, wm, wl):
    smem = pl.BlockSpec(memory_space=pltpu.SMEM)
    vmem = pl.BlockSpec(memory_space=pltpu.VMEM)
    return pl.pallas_call(
        score_kernel,
        out_shape=jax.ShapeDtypeStruct((1, NA, 8 * WB), F32),
        in_specs=[smem] * 4 + [vmem] * 7,
        out_specs=vmem,
        scratch_shapes=[
            pltpu.VMEM((27, 8, 128), F32),
            pltpu.VMEM((81 * 16, 128), F32),
            pltpu.VMEM((3, 128, 256), BF16),
            pltpu.VMEM((9, 256, 256), BF16),
            pltpu.VMEM((3, 192, 1536), BF16),
            pltpu.VMEM((NB + 2 * WB, 256), BF16),
            pltpu.VMEM((12 * WB, 768), BF16),
            pltpu.VMEM((BLOCKS, 3, 11 * WB, 256), BF16),
            pltpu.VMEM((10 * WB, 1536), BF16),
        ],
        compiler_params=pltpu.CompilerParams(vmem_limit_bytes=48 * 1024 * 1024),
        name="pair_scores",
    )(valid, b_first, b_middle, b_last, unit, own, other, copy_matrix(), wf, wm, wl)


def per_device(
    query_bank, ref_owner, target_feat, valid_rows, w_first, b_first, w_middle, b_middle, w_last, b_last
):
    n = lax.axis_size("pair")
    unit, other = exchange(ref_owner, query_bank, target_feat, n)
    wf = jnp.transpose(w_first, (1, 2, 3, 4, 5, 0)).reshape(27, 3, 16)
    wl = jnp.transpose(w_last, (0, 2, 3, 4, 5, 1)).reshape(27, 3, 16)
    wm = jnp.transpose(w_middle, (2, 3, 4, 5, 0, 1)).reshape(81, 16, 16)
    return score(valid_rows, b_first, b_middle, b_last, unit, target_feat, other, wf, wm, wl)


def solution(mesh):
    in_specs = (
        P("pair", None, None),
        P(),
        P("pair", None, "trow"),
        P("pair"),
        P(),
        P(),
        P(),
        P(),
        P(),
        P(),
    )
    out_specs = P("pair", None, "trow")
    return jax.shard_map(
        per_device, mesh=mesh, in_specs=in_specs, out_specs=out_specs, check_vma=False
    )
```

```python
import functools
import math

import jax
import jax.numpy as jnp
from jax import lax
from jax.experimental import pallas as pl
from jax.experimental.pallas import tpu as pltpu
from jax.sharding import PartitionSpec as P

MESH = pl.DeviceIdType.MESH
WB = 32
WA = 32
HB = 16
NB = HB * WB
NA = 64
EPS_NORM = 1e-06
EPS_PEAK = 1e-05
F32 = jnp.float32
BF16 = jnp.bfloat16

BLOCKS = 6
STEP = 6
HALF = 512


def nt(left, right):
    return lax.dot_general(left, right, (((1,), (1,)), ((), ())), preferred_element_type=F32)


def nn(left, right):
    return lax.dot_general(left, right, (((1,), (0,)), ((), ())), preferred_element_type=F32)


def iota(shape, dim):
    return lax.broadcasted_iota(jnp.int32, shape, dim)


def spread_rows(src_ref, tmp):
    tmp[...] = jnp.zeros_like(tmp)
    for t in range(27):
        tmp[t, 0:3, 0:16] = src_ref[t].astype(F32)
    flat = tmp[...].reshape(216, 128).astype(BF16)
    take = (iota((128, 128), 1) % 16 == iota((128, 128), 0)).astype(F32).astype(BF16)
    return nn(flat, take)


def bias_row(b_ref, used):
    lane = iota((1, 256), 1)
    row = jnp.zeros((1, 256), F32)
    for o in range(16):
        row = jnp.where(lane % 16 == o, b_ref[o], row)
    return jnp.where(lane < used, row, 0.0)


def prepare(wf_ref, wm_ref, wl_ref, tmp, spread, w1, w2, w3):
    spread[0:216, :] = spread_rows(wf_ref, tmp)
    row = iota((32, 128), 0)
    lane = iota((32, 128), 1)
    for tile in range(2):
        j_of = row // 2 - (tile * 4 + lane // 32)
        i_of = row % 2 - (lane // 16) % 2 + 1
        for k in range(3):
            for l in range(4):
                block = jnp.zeros((32, 128), F32)
                if l < 3:
                    for i in range(3):
                        for j in range(3):
                            t = (i * 3 + j) * 3 + k
                            value = spread[8 * t + l : 8 * t + l + 1, :]
                            block = jnp.where((j_of == j) & (i_of == i), value, block)
                w1[k, 32 * l : 32 * l + 32, 128 * tile : 128 * tile + 128] = block.astype(BF16)

    spread[0:216, :] = spread_rows(wl_ref, tmp)
    w3[...] = jnp.zeros_like(w3)
    odd1 = (iota((1, 128), 1) // 16) % 2 == 1
    for half in range(2):
        for tile in range(12):
            m, first = tile // 2, (tile % 2) * 4
            columns = [6 * m + q for q in range(first, first + 4) if q < STEP and 6 * m + q < WA]
            if not columns or columns[-1] < 16 * half - 1 or columns[0] > 16 * half + 16:
                continue
            q_of = first + iota((16, 128), 1) // 32
            c_in = 6 * m + q_of
            j_of = c_in - (16 * half + iota((16, 128), 0)) + 1
            j_of = jnp.where((q_of < STEP) & (c_in < WA), j_of, -1)
            for k in range(3):
                for l in range(3):
                    for ra in range(2):
                        block = jnp.zeros((16, 128), F32)
                        for j in range(3):
                            t0 = ((1 - ra) * 3 + j) * 3 + k
                            t1 = ((2 - ra) * 3 + j) * 3 + k
                            value = jnp.where(
                                odd1,
                                spread[8 * t1 + l : 8 * t1 + l + 1, :],
                                spread[8 * t0 + l : 8 * t0 + l + 1, :],
                            )
                            block = jnp.where(j_of == j, value, block)
                        at = 64 * l + 32 * ra + 16 * half
                        w3[k, at : at + 16, 128 * tile : 128 * tile + 128] = block.astype(BF16)

    take = (iota((16, 128), 1) % 16 == iota((16, 128), 0)).astype(F32).astype(BF16)
    spread[...] = nn(wm_ref[...].reshape(81 * 16, 16), take)
    odd = (iota((16, 128), 1) // 16) % 2 == 1
    p_of = iota((16, 128), 1) // 32
    for k in range(3):
        for l in range(3):
            w2[3 * k + l, 192:256, :] = jnp.zeros((64, 256), BF16)
            for ra in range(2):
                values = []
                for j in range(3):
                    t0 = (((1 - ra) * 3 + j) * 3 + k) * 3 + l
                    t1 = (((2 - ra) * 3 + j) * 3 + k) * 3 + l
                    values.append(
                        jnp.where(odd, spread[16 * t1 : 16 * t1 + 16, :], spread[16 * t0 : 16 * t0 + 16, :])
                    )
                for q in range(STEP):
                    for tile in range(2):
                        block = jnp.zeros((16, 128), F32)
                        for j in range(3):
                            block = jnp.where(p_of == q + j - 4 * tile, values[j], block)
                        at = 32 * q + 16 * ra
                        w2[3 * k + l, at : at + 16, 128 * tile : 128 * tile + 128] = block.astype(BF16)


def shifted(values, by, edge):
    rows = values.shape[0]
    moved = pltpu.roll(values, by % rows, 0)
    return jnp.where(iota(values.shape, 0) % WB == edge, 0.0, moved)


def copy_matrix(e_ref):
    for m in range(BLOCKS):
        source = iota((256, 128), 0)
        lane = iota((256, 128), 1)
        shift, inner = lane // 32, lane % 32
        column, ref_row = 6 * m - 2 + inner // 2, inner % 2
        used = (inner < 20) & (column >= 0) & (column < WA) & (shift < 3)
        hit = used & (source == shift * NA + ref_row * WA + column)
        e_ref[:, 128 * m : 128 * m + 128] = jnp.where(hit, 1.0, 0.0).astype(BF16)


def unit_slices(values, unit, plane, rows):
    values = values.astype(F32)
    scale = lax.rsqrt(jnp.sum(values * values, axis=1, keepdims=True) + EPS_NORM)
    normed = values * scale
    mine = jnp.where(plane == 0, normed[:, 0:HALF], normed[:, HALF : 2 * HALF])
    for s in range(32):
        g, t = s // 4, s % 4
        at = 8 * s
        unit[at // rows, at % rows : at % rows + 8, :] = mine[8 * g : 8 * g + 8, 128 * t : 128 * t + 128].astype(BF16)


def squares_of(feats, out_ref):
    values = feats.astype(F32)
    sums = jnp.sum(values * values, axis=1, keepdims=True)
    for t in range(4):
        wide = jnp.broadcast_to(sums[128 * t : 128 * t + 128], (128, 128))
        out_ref[t : t + 1, :] = jnp.transpose(wide)[0:1, :]


def kernel(
    sizes, owner_ref, valid_ref, bf_ref, bm_ref, bl_ref, q_hbm, t_hbm, wf_hbm, wm_hbm, wl_hbm,
    out_ref,
    q_ref, t_ref, wf_ref, wm_ref, wl_ref, unit, recv_a, cand, recv_b, piece, gath, sq_own, sq_oth, part, part_oth,
    tmp, spread, w1, w2, w3, e_ref, vbuf, xbuf, h1, h2, loads, sems,
):
    group, depth, inner, rows = sizes
    me = lax.axis_index("pair")
    plane = lax.axis_index("trow")
    z = lax.rem(me // inner, depth)
    g = (me // (inner * depth)) * inner + lax.rem(me, inner)

    def at(g_of, z_of):
        return ((g_of // inner) * depth + z_of) * inner + lax.rem(g_of, inner)

    def in_group(o):
        return at(lax.rem(g + o, group), z)

    def along(o):
        return at(g, lax.rem(z + o, depth))

    barrier = pltpu.get_barrier_semaphore()

    def greet(pair, trow):
        pl.semaphore_signal(barrier, inc=1, device_id=(pair, trow), device_id_type=MESH)

    pl.loop(1, depth)(lambda o: greet(along(o), plane))
    if group > 1:
        pl.loop(1, group)(lambda o: greet(in_group(o), plane))
    greet(me, 1 - plane)

    local = [
        pltpu.make_async_copy(src, dst, loads.at[i])
        for i, (src, dst) in enumerate(
            ((q_hbm.at[0], q_ref), (wf_hbm, wf_ref), (wl_hbm, wl_ref), (wm_hbm, wm_ref), (t_hbm.at[0], t_ref))
        )
    ]
    for copy in local:
        copy.start()
    copy_matrix(e_ref)
    local[0].wait()
    unit_slices(q_ref[...], unit, plane, rows)
    for copy in local[1:4]:
        copy.wait()
    prepare(wf_ref, wm_ref, wl_ref, tmp, spread, w1, w2, w3)
    local[4].wait()
    squares_of(t_ref[...], sq_own)

    pl.semaphore_wait(barrier, (depth - 1) + (group - 1) + 1)

    def send(src, dst, k, pair, trow):
        copy = pltpu.make_async_remote_copy(
            src_ref=src,
            dst_ref=dst,
            send_sem=sems.at[2 * k],
            recv_sem=sems.at[2 * k + 1],
            device_id=(pair, trow),
            device_id_type=MESH,
        )
        copy.start()
        return copy

    def wait(ref, k):
        pltpu.make_async_copy(ref, ref, sems.at[k]).wait()

    owner = owner_ref[0]
    owner_g = (owner // (inner * depth)) * inner + lax.rem(owner, inner)
    owner_z = lax.rem(owner // inner, depth)

    if group > 1:
        pl.loop(1, group)(
            lambda o: send(unit.at[lax.rem(g + o, group)], recv_a.at[g], 0, in_group(o), plane) and None
        )
    squares = send(sq_own, sq_oth, 4, me, 1 - plane)
    recv_a[g] = unit[g]
    if group > 1:
        wait(recv_a.at[pl.ds(0, group - 1)], 1)
    chosen = recv_a[owner_g]
    cand[...] = chosen
    recv_b[z] = chosen

    pl.loop(1, depth)(lambda o: send(cand, recv_b.at[z], 1, along(o), plane) and None)
    wait(recv_b.at[pl.ds(0, depth - 1)], 3)
    chosen = recv_b[owner_z]
    piece[...] = chosen
    gath[g] = chosen

    if group > 1:
        pl.loop(1, group)(lambda o: send(piece, gath.at[g], 2, in_group(o), plane) and None)
        wait(gath.at[pl.ds(0, group - 1)], 5)
    lines = []
    for line in range(8):
        tiles = []
        for t in range(4):
            first = 8 * (4 * line + t)
            tiles.append(gath[first // rows, first % rows : first % rows + 8, :].astype(F32))
        lines.append(jnp.concatenate(tiles, axis=1))
    window = jnp.concatenate(lines, axis=0).astype(BF16)

    blank = jnp.zeros((NA, HALF), BF16)
    part[...] = nt(t_ref[0:256, :], jnp.concatenate([window, blank], axis=0)) + nt(
        t_ref[256:512, :], jnp.concatenate([blank, window], axis=0)
    )
    partial = send(part, part_oth, 3, me, 1 - plane)

    b1 = bias_row(bf_ref, 256)
    b2 = bias_row(bm_ref, 32 * STEP)
    squares.wait()
    columns = []
    for t in range(4):
        total = sq_own[t : t + 1, :] + sq_oth[t : t + 1, :]
        columns.append(jnp.transpose(jnp.broadcast_to(total, (128, 128))))
    inverse = lax.rsqrt(jnp.concatenate(columns, axis=0) + EPS_NORM)
    live = iota((NB, 128), 0) // WB < valid_ref[0]

    partial.wait()
    both = part[...] + part_oth[...]
    swapped = pltpu.roll(both, 64, 1)
    low = iota((256, 128), 1) < 64
    raw = jnp.concatenate([jnp.where(low, both, swapped), jnp.where(low, swapped, both)], axis=0)
    corr = jnp.where(live, math.sqrt(1024) * raw * inverse, 0.0)
    magnitude = jnp.abs(corr)
    peak_query = jnp.max(magnitude, axis=1, keepdims=True)
    peak_target = jnp.max(magnitude, axis=0, keepdims=True)
    volume = corr * (corr * (1.0 / (peak_query + EPS_PEAK))) * (corr * (1.0 / (peak_target + EPS_PEAK)))
    vbuf[0:WB, :] = jnp.zeros((WB, 256), BF16)
    vbuf[WB + NB : 2 * WB + NB, :] = jnp.zeros((WB, 256), BF16)
    low = iota((NB, 128), 1) < 64
    vbuf[WB : WB + NB, 0:128] = jnp.where(low, shifted(volume, 1, 0), volume).astype(BF16)
    vbuf[WB : WB + NB, 128:256] = shifted(volume, -1, WB - 1).astype(BF16)
    start = pl.multiple_of(plane * (6 * WB), 6 * WB)
    xbuf[...] = nn(vbuf[pl.ds(start, 12 * WB), :], e_ref[...]).astype(BF16)

    pad = pl.multiple_of((1 - plane) * WB, WB)

    lane = iota((10 * WB, 256), 1)
    for m in range(BLOCKS):
        acc = nn(xbuf[0 : 10 * WB, 128 * m : 128 * m + 128], w1[0])
        for k in (1, 2):
            acc = acc + nn(xbuf[WB * k : WB * k + 10 * WB, 128 * m : 128 * m + 128], w1[k])
        hidden = jnp.maximum(acc + b1, 0.0)
        if m == 0:
            hidden = jnp.where(lane < 32, 0.0, hidden)
        if m == BLOCKS - 1:
            hidden = jnp.where(lane >= 32 * (WA - 6 * m + 1), 0.0, hidden)
        zero = jnp.zeros((WB, 256), BF16)
        edge = pl.multiple_of(plane * (10 * WB), WB)
        for l in range(3):
            h1[m, l, pl.ds(edge, WB), :] = zero
        h1[m, 0, pl.ds(pad, 10 * WB), :] = shifted(hidden, 1, 0).astype(BF16)
        h1[m, 1, pl.ds(pad, 10 * WB), :] = hidden.astype(BF16)
        h1[m, 2, pl.ds(pad, 10 * WB), :] = shifted(hidden, -1, WB - 1).astype(BF16)

    edge = pl.multiple_of(plane * (9 * WB), WB)
    for m in range(BLOCKS):
        acc = jnp.zeros((9 * WB, 256), F32)
        for k in range(3):
            for l in range(3):
                acc = acc + nt(h1[m, l, WB * k : WB * k + 9 * WB, :], w2[3 * k + l])
        hidden = jnp.maximum(acc + b2, 0.0)
        h2[pl.ds(edge, WB), 256 * m : 256 * m + 256] = jnp.zeros((WB, 256), BF16)
        h2[pl.ds(pad, 9 * WB), 256 * m : 256 * m + 256] = hidden.astype(BF16)

    acc = nt(w3[0], h2[0 : 8 * WB, :])
    for k in (1, 2):
        acc = acc + nt(w3[k], h2[WB * k : WB * k + 8 * WB, :])
    column = iota((NA, 8 * WB), 1) % WB
    result = acc[NA : 2 * NA]
    result = result + jnp.where(column == 0, 0.0, pltpu.roll(acc[0:NA], 1, 1))
    result = result + jnp.where(column == WB - 1, 0.0, pltpu.roll(acc[2 * NA : 3 * NA], 8 * WB - 1, 1))
    result = result + bl_ref[0]
    row = plane * 8 + iota((NA, 8 * WB), 1) // WB
    out_ref[0] = jnp.where(row < valid_ref[0], result, 0.0)

    if group > 1:
        wait(recv_a.at[pl.ds(0, group - 1)], 0)
        wait(gath.at[pl.ds(0, group - 1)], 4)
    wait(recv_b.at[pl.ds(0, depth - 1)], 2)


def layout_of(n):
    inner = min(8, max(1, n // 2))
    depth = min(8, n // inner)
    group = n // depth
    return group, depth, inner, 256 // group


def score(owner, valid, b_first, b_middle, b_last, bank, feats, wf, wm, wl, n):
    smem = pl.BlockSpec(memory_space=pltpu.SMEM)
    hbm = pl.BlockSpec(memory_space=pltpu.HBM)
    sizes = layout_of(n)
    group, depth, _, rows = sizes
    return pl.pallas_call(
        functools.partial(kernel, sizes),
        out_shape=jax.ShapeDtypeStruct((1, NA, 8 * WB), F32),
        in_specs=[smem] * 5 + [hbm] * 5,
        out_specs=pl.BlockSpec(memory_space=pltpu.VMEM),
        scratch_shapes=[
            pltpu.VMEM((NA, 2 * HALF), BF16),
            pltpu.VMEM((NB, HALF), BF16),
            pltpu.VMEM((27, 3, 16), BF16),
            pltpu.VMEM((81, 16, 16), BF16),
            pltpu.VMEM((27, 3, 16), BF16),
            pltpu.VMEM((group, rows, 128), BF16),
            pltpu.VMEM((group, rows, 128), BF16),
            pltpu.VMEM((rows, 128), BF16),
            pltpu.VMEM((depth, rows, 128), BF16),
            pltpu.VMEM((rows, 128), BF16),
            pltpu.VMEM((group, rows, 128), BF16),
            pltpu.VMEM((8, 128), F32),
            pltpu.VMEM((8, 128), F32),
            pltpu.VMEM((256, 128), F32),
            pltpu.VMEM((256, 128), F32),
            pltpu.VMEM((27, 8, 128), F32),
            pltpu.VMEM((81 * 16, 128), F32),
            pltpu.VMEM((3, 128, 256), BF16),
            pltpu.VMEM((9, 256, 256), BF16),
            pltpu.VMEM((3, 192, 1536), BF16),
            pltpu.VMEM((256, 768), BF16),
            pltpu.VMEM((NB + 2 * WB, 256), BF16),
            pltpu.VMEM((12 * WB, 768), BF16),
            pltpu.VMEM((BLOCKS, 3, 11 * WB, 256), BF16),
            pltpu.VMEM((10 * WB, 1536), BF16),
            pltpu.SemaphoreType.DMA((5,)),
            pltpu.SemaphoreType.DMA((10,)),
        ],
        compiler_params=pltpu.CompilerParams(
            collective_id=0, has_side_effects=True, vmem_limit_bytes=48 * 1024 * 1024
        ),
        name="pair_scores",
    )(owner, valid, b_first, b_middle, b_last, bank, feats, wf, wm, wl)


def per_device(
    query_bank, ref_owner, target_feat, valid_rows, w_first, b_first, w_middle, b_middle, w_last, b_last
):
    wf = jnp.transpose(w_first, (1, 2, 3, 4, 5, 0)).reshape(27, 3, 16)
    wl = jnp.transpose(w_last, (0, 2, 3, 4, 5, 1)).reshape(27, 3, 16)
    wm = jnp.transpose(w_middle, (2, 3, 4, 5, 0, 1)).reshape(81, 16, 16)
    n = lax.axis_size("pair")
    return score(ref_owner, valid_rows, b_first, b_middle, b_last, query_bank, target_feat, wf, wm, wl, n)


def solution(mesh):
    in_specs = (
        P("pair", None, None),
        P(),
        P("pair", None, "trow"),
        P("pair"),
        P(),
        P(),
        P(),
        P(),
        P(),
        P(),
    )
    out_specs = P("pair", None, "trow")
    return jax.shard_map(
        per_device, mesh=mesh, in_specs=in_specs, out_specs=out_specs, check_vma=False
    )
```

```python
import functools
import math

import jax
import jax.numpy as jnp
from jax import lax
from jax.experimental import pallas as pl
from jax.experimental.pallas import tpu as pltpu
from jax.sharding import PartitionSpec as P

MESH = pl.DeviceIdType.MESH
WB = 32
WA = 32
HB = 16
NB = HB * WB
NA = 64
EPS_NORM = 1e-06
EPS_PEAK = 1e-05
F32 = jnp.float32
BF16 = jnp.bfloat16

BLOCKS = 6
STEP = 6
HALF = 512


def nt(left, right):
    return lax.dot_general(left, right, (((1,), (1,)), ((), ())), preferred_element_type=F32)


def nn(left, right):
    return lax.dot_general(left, right, (((1,), (0,)), ((), ())), preferred_element_type=F32)


def iota(shape, dim):
    return lax.broadcasted_iota(jnp.int32, shape, dim)


def spread_rows(src_ref, tmp):
    tmp[...] = jnp.zeros_like(tmp)
    for t in range(27):
        tmp[t, 0:3, 0:16] = src_ref[t].astype(F32)
    flat = tmp[...].reshape(216, 128).astype(BF16)
    take = (iota((128, 128), 1) % 16 == iota((128, 128), 0)).astype(F32).astype(BF16)
    return nn(flat, take)


def bias_row(b_ref, used):
    lane = iota((1, 256), 1)
    row = jnp.zeros((1, 256), F32)
    for o in range(16):
        row = jnp.where(lane % 16 == o, b_ref[o], row)
    return jnp.where(lane < used, row, 0.0)


def prepare(wf_ref, wm_ref, wl_ref, tmp, spread, w1, w2, w3):
    spread[0:216, :] = spread_rows(wf_ref, tmp)
    row = iota((32, 128), 0)
    lane = iota((32, 128), 1)
    for tile in range(2):
        j_of = row // 2 - (tile * 4 + lane // 32)
        i_of = row % 2 - (lane // 16) % 2 + 1
        for k in range(3):
            for l in range(4):
                block = jnp.zeros((32, 128), F32)
                if l < 3:
                    for i in range(3):
                        for j in range(3):
                            t = (i * 3 + j) * 3 + k
                            value = spread[8 * t + l : 8 * t + l + 1, :]
                            block = jnp.where((j_of == j) & (i_of == i), value, block)
                w1[k, 32 * l : 32 * l + 32, 128 * tile : 128 * tile + 128] = block.astype(BF16)

    spread[0:216, :] = spread_rows(wl_ref, tmp)
    w3[...] = jnp.zeros_like(w3)
    odd1 = (iota((1, 128), 1) // 16) % 2 == 1
    for half in range(2):
        for tile in range(12):
            m, first = tile // 2, (tile % 2) * 4
            columns = [6 * m + q for q in range(first, first + 4) if q < STEP and 6 * m + q < WA]
            if not columns or columns[-1] < 16 * half - 1 or columns[0] > 16 * half + 16:
                continue
            q_of = first + iota((16, 128), 1) // 32
            c_in = 6 * m + q_of
            j_of = c_in - (16 * half + iota((16, 128), 0)) + 1
            j_of = jnp.where((q_of < STEP) & (c_in < WA), j_of, -1)
            for k in range(3):
                for l in range(3):
                    for ra in range(2):
                        block = jnp.zeros((16, 128), F32)
                        for j in range(3):
                            t0 = ((1 - ra) * 3 + j) * 3 + k
                            t1 = ((2 - ra) * 3 + j) * 3 + k
                            value = jnp.where(
                                odd1,
                                spread[8 * t1 + l : 8 * t1 + l + 1, :],
                                spread[8 * t0 + l : 8 * t0 + l + 1, :],
                            )
                            block = jnp.where(j_of == j, value, block)
                        at = 64 * l + 32 * ra + 16 * half
                        w3[k, at : at + 16, 128 * tile : 128 * tile + 128] = block.astype(BF16)

    take = (iota((16, 128), 1) % 16 == iota((16, 128), 0)).astype(F32).astype(BF16)
    spread[...] = nn(wm_ref[...].reshape(81 * 16, 16), take)
    odd = (iota((16, 128), 1) // 16) % 2 == 1
    p_of = iota((16, 128), 1) // 32
    for k in range(3):
        for l in range(3):
            w2[3 * k + l, 192:256, :] = jnp.zeros((64, 256), BF16)
            for ra in range(2):
                values = []
                for j in range(3):
                    t0 = (((1 - ra) * 3 + j) * 3 + k) * 3 + l
                    t1 = (((2 - ra) * 3 + j) * 3 + k) * 3 + l
                    values.append(
                        jnp.where(odd, spread[16 * t1 : 16 * t1 + 16, :], spread[16 * t0 : 16 * t0 + 16, :])
                    )
                for q in range(STEP):
                    for tile in range(2):
                        block = jnp.zeros((16, 128), F32)
                        for j in range(3):
                            block = jnp.where(p_of == q + j - 4 * tile, values[j], block)
                        at = 32 * q + 16 * ra
                        w2[3 * k + l, at : at + 16, 128 * tile : 128 * tile + 128] = block.astype(BF16)


def shifted(values, by, edge):
    rows = values.shape[0]
    moved = pltpu.roll(values, by % rows, 0)
    return jnp.where(iota(values.shape, 0) % WB == edge, 0.0, moved)


def copy_matrix(e_ref):
    for m in range(BLOCKS):
        source = iota((256, 128), 0)
        lane = iota((256, 128), 1)
        shift, inner = lane // 32, lane % 32
        column, ref_row = 6 * m - 2 + inner // 2, inner % 2
        used = (inner < 20) & (column >= 0) & (column < WA) & (shift < 3)
        hit = used & (source == shift * NA + ref_row * WA + column)
        e_ref[:, 128 * m : 128 * m + 128] = jnp.where(hit, 1.0, 0.0).astype(BF16)


def unit_slices(values, unit, plane, rows):
    values = values.astype(F32)
    scale = lax.rsqrt(jnp.sum(values * values, axis=1, keepdims=True) + EPS_NORM)
    normed = values * scale
    mine = jnp.where(plane == 0, normed[:, 0:HALF], normed[:, HALF : 2 * HALF])
    for s in range(32):
        g, t = s // 4, s % 4
        at = 8 * s
        unit[at // rows, at % rows : at % rows + 8, :] = mine[8 * g : 8 * g + 8, 128 * t : 128 * t + 128].astype(BF16)


def squares_of(feats, out_ref):
    values = feats.astype(F32)
    sums = jnp.sum(values * values, axis=1, keepdims=True)
    for t in range(4):
        wide = jnp.broadcast_to(sums[128 * t : 128 * t + 128], (128, 128))
        out_ref[t : t + 1, :] = jnp.transpose(wide)[0:1, :]


def kernel(
    sizes, owner_hbm, valid_hbm, bf_hbm, bm_hbm, bl_hbm, q_hbm, t_hbm, wf_hbm, wm_hbm, wl_hbm,
    out_ref,
    owner_ref, valid_ref, bf_ref, bm_ref, bl_ref, q_ref, t_ref, wf_ref, wm_ref, wl_ref, unit, recv_a, cand, recv_b, piece, gath, sq_own, sq_oth, part, part_oth,
    tmp, spread, w1, w2, w3, e_ref, vbuf, xbuf, h1, h2, loads, sems,
):
    group, depth, inner, rows = sizes
    me = lax.axis_index("pair")
    plane = lax.axis_index("trow")
    z = lax.rem(me // inner, depth)
    g = (me // (inner * depth)) * inner + lax.rem(me, inner)

    def at(g_of, z_of):
        return ((g_of // inner) * depth + z_of) * inner + lax.rem(g_of, inner)

    def in_group(o):
        return at(lax.rem(g + o, group), z)

    def along(o):
        return at(g, lax.rem(z + o, depth))

    barrier = pltpu.get_barrier_semaphore()

    def greet(pair, trow):
        pl.semaphore_signal(barrier, inc=1, device_id=(pair, trow), device_id_type=MESH)

    pl.loop(1, depth)(lambda o: greet(along(o), plane))
    if group > 1:
        pl.loop(1, group)(lambda o: greet(in_group(o), plane))
    greet(me, 1 - plane)

    local = [
        pltpu.make_async_copy(src, dst, loads.at[i])
        for i, (src, dst) in enumerate(
            (
                (q_hbm.at[0], q_ref),
                (wf_hbm, wf_ref),
                (wl_hbm, wl_ref),
                (wm_hbm, wm_ref),
                (t_hbm.at[0], t_ref),
                (owner_hbm, owner_ref),
                (valid_hbm, valid_ref),
                (bf_hbm, bf_ref),
                (bm_hbm, bm_ref),
                (bl_hbm, bl_ref),
            )
        )
    ]
    for copy in local:
        copy.start()
    copy_matrix(e_ref)
    local[0].wait()
    unit_slices(q_ref[...], unit, plane, rows)
    for copy in local[1:4]:
        copy.wait()
    prepare(wf_ref, wm_ref, wl_ref, tmp, spread, w1, w2, w3)
    for copy in local[4:]:
        copy.wait()
    squares_of(t_ref[...], sq_own)

    pl.semaphore_wait(barrier, (depth - 1) + (group - 1) + 1)

    def send(src, dst, k, pair, trow):
        copy = pltpu.make_async_remote_copy(
            src_ref=src,
            dst_ref=dst,
            send_sem=sems.at[2 * k],
            recv_sem=sems.at[2 * k + 1],
            device_id=(pair, trow),
            device_id_type=MESH,
        )
        copy.start()
        return copy

    def wait(ref, k):
        pltpu.make_async_copy(ref, ref, sems.at[k]).wait()

    owner = owner_ref[0]
    owner_g = (owner // (inner * depth)) * inner + lax.rem(owner, inner)
    owner_z = lax.rem(owner // inner, depth)

    if group > 1:
        pl.loop(1, group)(
            lambda o: send(unit.at[lax.rem(g + o, group)], recv_a.at[g], 0, in_group(o), plane) and None
        )
    squares = send(sq_own, sq_oth, 4, me, 1 - plane)
    recv_a[g] = unit[g]
    if group > 1:
        wait(recv_a.at[pl.ds(0, group - 1)], 1)
    chosen = recv_a[owner_g]
    cand[...] = chosen
    recv_b[z] = chosen

    pl.loop(1, depth)(lambda o: send(cand, recv_b.at[z], 1, along(o), plane) and None)
    wait(recv_b.at[pl.ds(0, depth - 1)], 3)
    chosen = recv_b[owner_z]
    piece[...] = chosen
    gath[g] = chosen

    if group > 1:
        pl.loop(1, group)(lambda o: send(piece, gath.at[g], 2, in_group(o), plane) and None)
        wait(gath.at[pl.ds(0, group - 1)], 5)
    lines = []
    for line in range(8):
        tiles = []
        for t in range(4):
            first = 8 * (4 * line + t)
            tiles.append(gath[first // rows, first % rows : first % rows + 8, :].astype(F32))
        lines.append(jnp.concatenate(tiles, axis=1))
    window = jnp.concatenate(lines, axis=0).astype(BF16)

    blank = jnp.zeros((NA, HALF), BF16)
    part[...] = nt(t_ref[0:256, :], jnp.concatenate([window, blank], axis=0)) + nt(
        t_ref[256:512, :], jnp.concatenate([blank, window], axis=0)
    )
    partial = send(part, part_oth, 3, me, 1 - plane)

    b1 = bias_row(bf_ref, 256)
    b2 = bias_row(bm_ref, 32 * STEP)
    squares.wait()
    columns = []
    for t in range(4):
        total = sq_own[t : t + 1, :] + sq_oth[t : t + 1, :]
        columns.append(jnp.transpose(jnp.broadcast_to(total, (128, 128))))
    inverse = lax.rsqrt(jnp.concatenate(columns, axis=0) + EPS_NORM)
    live = iota((NB, 128), 0) // WB < valid_ref[0]

    partial.wait()
    both = part[...] + part_oth[...]
    swapped = pltpu.roll(both, 64, 1)
    low = iota((256, 128), 1) < 64
    raw = jnp.concatenate([jnp.where(low, both, swapped), jnp.where(low, swapped, both)], axis=0)
    corr = jnp.where(live, math.sqrt(1024) * raw * inverse, 0.0)
    magnitude = jnp.abs(corr)
    peak_query = jnp.max(magnitude, axis=1, keepdims=True)
    peak_target = jnp.max(magnitude, axis=0, keepdims=True)
    volume = corr * (corr * (1.0 / (peak_query + EPS_PEAK))) * (corr * (1.0 / (peak_target + EPS_PEAK)))
    vbuf[0:WB, :] = jnp.zeros((WB, 256), BF16)
    vbuf[WB + NB : 2 * WB + NB, :] = jnp.zeros((WB, 256), BF16)
    low = iota((NB, 128), 1) < 64
    vbuf[WB : WB + NB, 0:128] = jnp.where(low, shifted(volume, 1, 0), volume).astype(BF16)
    vbuf[WB : WB + NB, 128:256] = shifted(volume, -1, WB - 1).astype(BF16)
    start = pl.multiple_of(plane * (6 * WB), 6 * WB)
    xbuf[...] = nn(vbuf[pl.ds(start, 12 * WB), :], e_ref[...]).astype(BF16)

    pad = pl.multiple_of((1 - plane) * WB, WB)

    lane = iota((10 * WB, 256), 1)
    for m in range(BLOCKS):
        acc = nn(xbuf[0 : 10 * WB, 128 * m : 128 * m + 128], w1[0])
        for k in (1, 2):
            acc = acc + nn(xbuf[WB * k : WB * k + 10 * WB, 128 * m : 128 * m + 128], w1[k])
        hidden = jnp.maximum(acc + b1, 0.0)
        if m == 0:
            hidden = jnp.where(lane < 32, 0.0, hidden)
        if m == BLOCKS - 1:
            hidden = jnp.where(lane >= 32 * (WA - 6 * m + 1), 0.0, hidden)
        zero = jnp.zeros((WB, 256), BF16)
        edge = pl.multiple_of(plane * (10 * WB), WB)
        for l in range(3):
            h1[m, l, pl.ds(edge, WB), :] = zero
        h1[m, 0, pl.ds(pad, 10 * WB), :] = shifted(hidden, 1, 0).astype(BF16)
        h1[m, 1, pl.ds(pad, 10 * WB), :] = hidden.astype(BF16)
        h1[m, 2, pl.ds(pad, 10 * WB), :] = shifted(hidden, -1, WB - 1).astype(BF16)

    edge = pl.multiple_of(plane * (9 * WB), WB)
    for m in range(BLOCKS):
        acc = jnp.zeros((9 * WB, 256), F32)
        for k in range(3):
            for l in range(3):
                acc = acc + nt(h1[m, l, WB * k : WB * k + 9 * WB, :], w2[3 * k + l])
        hidden = jnp.maximum(acc + b2, 0.0)
        h2[pl.ds(edge, WB), 256 * m : 256 * m + 256] = jnp.zeros((WB, 256), BF16)
        h2[pl.ds(pad, 9 * WB), 256 * m : 256 * m + 256] = hidden.astype(BF16)

    acc = nt(w3[0], h2[0 : 8 * WB, :])
    for k in (1, 2):
        acc = acc + nt(w3[k], h2[WB * k : WB * k + 8 * WB, :])
    column = iota((NA, 8 * WB), 1) % WB
    result = acc[NA : 2 * NA]
    result = result + jnp.where(column == 0, 0.0, pltpu.roll(acc[0:NA], 1, 1))
    result = result + jnp.where(column == WB - 1, 0.0, pltpu.roll(acc[2 * NA : 3 * NA], 8 * WB - 1, 1))
    result = result + bl_ref[0]
    row = plane * 8 + iota((NA, 8 * WB), 1) // WB
    out_ref[0] = jnp.where(row < valid_ref[0], result, 0.0)

    if group > 1:
        wait(recv_a.at[pl.ds(0, group - 1)], 0)
        wait(gath.at[pl.ds(0, group - 1)], 4)
    wait(recv_b.at[pl.ds(0, depth - 1)], 2)


def layout_of(n):
    inner = min(8, max(1, n // 2))
    depth = min(8, n // inner)
    group = n // depth
    return group, depth, inner, 256 // group


def score(owner, valid, b_first, b_middle, b_last, bank, feats, wf, wm, wl, n):
    hbm = pl.BlockSpec(memory_space=pltpu.HBM)
    sizes = layout_of(n)
    group, depth, _, rows = sizes
    return pl.pallas_call(
        functools.partial(kernel, sizes),
        out_shape=pltpu.VMEM((1, NA, 8 * WB), F32),
        in_specs=[hbm] * 10,
        out_specs=pl.BlockSpec(memory_space=pltpu.VMEM),
        scratch_shapes=[
            pltpu.SMEM((1,), jnp.int32),
            pltpu.SMEM((1,), jnp.int32),
            pltpu.SMEM((16,), F32),
            pltpu.SMEM((16,), F32),
            pltpu.SMEM((1,), F32),
            pltpu.VMEM((NA, 2 * HALF), BF16),
            pltpu.VMEM((NB, HALF), BF16),
            pltpu.VMEM((27, 3, 16), BF16),
            pltpu.VMEM((81, 16, 16), BF16),
            pltpu.VMEM((27, 3, 16), BF16),
            pltpu.VMEM((group, rows, 128), BF16),
            pltpu.VMEM((group, rows, 128), BF16),
            pltpu.VMEM((rows, 128), BF16),
            pltpu.VMEM((depth, rows, 128), BF16),
            pltpu.VMEM((rows, 128), BF16),
            pltpu.VMEM((group, rows, 128), BF16),
            pltpu.VMEM((8, 128), F32),
            pltpu.VMEM((8, 128), F32),
            pltpu.VMEM((256, 128), F32),
            pltpu.VMEM((256, 128), F32),
            pltpu.VMEM((27, 8, 128), F32),
            pltpu.VMEM((81 * 16, 128), F32),
            pltpu.VMEM((3, 128, 256), BF16),
            pltpu.VMEM((9, 256, 256), BF16),
            pltpu.VMEM((3, 192, 1536), BF16),
            pltpu.VMEM((256, 768), BF16),
            pltpu.VMEM((NB + 2 * WB, 256), BF16),
            pltpu.VMEM((12 * WB, 768), BF16),
            pltpu.VMEM((BLOCKS, 3, 11 * WB, 256), BF16),
            pltpu.VMEM((10 * WB, 1536), BF16),
            pltpu.SemaphoreType.DMA((10,)),
            pltpu.SemaphoreType.DMA((10,)),
        ],
        compiler_params=pltpu.CompilerParams(
            collective_id=0, has_side_effects=True, vmem_limit_bytes=60 * 1024 * 1024
        ),
        name="pair_scores",
    )(owner, valid, b_first, b_middle, b_last, bank, feats, wf, wm, wl)


def per_device(
    query_bank, ref_owner, target_feat, valid_rows, w_first, b_first, w_middle, b_middle, w_last, b_last
):
    wf = jnp.transpose(w_first, (1, 2, 3, 4, 5, 0)).reshape(27, 3, 16)
    wl = jnp.transpose(w_last, (0, 2, 3, 4, 5, 1)).reshape(27, 3, 16)
    wm = jnp.transpose(w_middle, (2, 3, 4, 5, 0, 1)).reshape(81, 16, 16)
    n = lax.axis_size("pair")
    return score(ref_owner, valid_rows, b_first, b_middle, b_last, query_bank, target_feat, wf, wm, wl, n)


def solution(mesh):
    in_specs = (
        P("pair", None, None),
        P(),
        P("pair", None, "trow"),
        P("pair"),
        P(),
        P(),
        P(),
        P(),
        P(),
        P(),
    )
    out_specs = P("pair", None, "trow")
    return jax.shard_map(
        per_device, mesh=mesh, in_specs=in_specs, out_specs=out_specs, check_vma=False
    )
```

```python
import functools
import math

import jax
import jax.numpy as jnp
from jax import lax
from jax.experimental import pallas as pl
from jax.experimental.pallas import tpu as pltpu
from jax.sharding import PartitionSpec as P

MESH = pl.DeviceIdType.MESH
WB = 32
WA = 32
HB = 16
NB = HB * WB
NA = 64
EPS_NORM = 1e-06
EPS_PEAK = 1e-05
F32 = jnp.float32
BF16 = jnp.bfloat16

BLOCKS = 6
STEP = 6
HALF = 512
CHUNKS = 2


def nt(left, right):
    return lax.dot_general(left, right, (((1,), (1,)), ((), ())), preferred_element_type=F32)


def nn(left, right):
    return lax.dot_general(left, right, (((1,), (0,)), ((), ())), preferred_element_type=F32)


def iota(shape, dim):
    return lax.broadcasted_iota(jnp.int32, shape, dim)


def spread_rows(src_ref, tmp):
    tmp[...] = jnp.zeros_like(tmp)
    for t in range(27):
        tmp[t, 0:3, 0:16] = src_ref[t].astype(F32)
    flat = tmp[...].reshape(216, 128).astype(BF16)
    take = (iota((128, 128), 1) % 16 == iota((128, 128), 0)).astype(F32).astype(BF16)
    return nn(flat, take)


def bias_row(b_ref, used):
    lane = iota((1, 256), 1)
    row = jnp.zeros((1, 256), F32)
    for o in range(16):
        row = jnp.where(lane % 16 == o, b_ref[o], row)
    return jnp.where(lane < used, row, 0.0)


def prepare(wf_ref, wm_ref, wl_ref, tmp, spread, w1, w2, w3):
    spread[0:216, :] = spread_rows(wf_ref, tmp)
    row = iota((32, 128), 0)
    lane = iota((32, 128), 1)
    for tile in range(2):
        j_of = row // 2 - (tile * 4 + lane // 32)
        i_of = row % 2 - (lane // 16) % 2 + 1
        for k in range(3):
            for l in range(4):
                block = jnp.zeros((32, 128), F32)
                if l < 3:
                    for i in range(3):
                        for j in range(3):
                            t = (i * 3 + j) * 3 + k
                            value = spread[8 * t + l : 8 * t + l + 1, :]
                            block = jnp.where((j_of == j) & (i_of == i), value, block)
                w1[k, 32 * l : 32 * l + 32, 128 * tile : 128 * tile + 128] = block.astype(BF16)

    spread[0:216, :] = spread_rows(wl_ref, tmp)
    w3[...] = jnp.zeros_like(w3)
    odd1 = (iota((1, 128), 1) // 16) % 2 == 1
    for half in range(2):
        for tile in range(12):
            m, first = tile // 2, (tile % 2) * 4
            columns = [6 * m + q for q in range(first, first + 4) if q < STEP and 6 * m + q < WA]
            if not columns or columns[-1] < 16 * half - 1 or columns[0] > 16 * half + 16:
                continue
            q_of = first + iota((16, 128), 1) // 32
            c_in = 6 * m + q_of
            j_of = c_in - (16 * half + iota((16, 128), 0)) + 1
            j_of = jnp.where((q_of < STEP) & (c_in < WA), j_of, -1)
            for k in range(3):
                for l in range(3):
                    for ra in range(2):
                        block = jnp.zeros((16, 128), F32)
                        for j in range(3):
                            t0 = ((1 - ra) * 3 + j) * 3 + k
                            t1 = ((2 - ra) * 3 + j) * 3 + k
                            value = jnp.where(
                                odd1,
                                spread[8 * t1 + l : 8 * t1 + l + 1, :],
                                spread[8 * t0 + l : 8 * t0 + l + 1, :],
                            )
                            block = jnp.where(j_of == j, value, block)
                        at = 64 * l + 32 * ra + 16 * half
                        w3[k, at : at + 16, 128 * tile : 128 * tile + 128] = block.astype(BF16)

    take = (iota((16, 128), 1) % 16 == iota((16, 128), 0)).astype(F32).astype(BF16)
    spread[...] = nn(wm_ref[...].reshape(81 * 16, 16), take)
    odd = (iota((16, 128), 1) // 16) % 2 == 1
    p_of = iota((16, 128), 1) // 32
    for k in range(3):
        for l in range(3):
            w2[3 * k + l, 192:256, :] = jnp.zeros((64, 256), BF16)
            for ra in range(2):
                values = []
                for j in range(3):
                    t0 = (((1 - ra) * 3 + j) * 3 + k) * 3 + l
                    t1 = (((2 - ra) * 3 + j) * 3 + k) * 3 + l
                    values.append(
                        jnp.where(odd, spread[16 * t1 : 16 * t1 + 16, :], spread[16 * t0 : 16 * t0 + 16, :])
                    )
                for q in range(STEP):
                    for tile in range(2):
                        block = jnp.zeros((16, 128), F32)
                        for j in range(3):
                            block = jnp.where(p_of == q + j - 4 * tile, values[j], block)
                        at = 32 * q + 16 * ra
                        w2[3 * k + l, at : at + 16, 128 * tile : 128 * tile + 128] = block.astype(BF16)


def shifted(values, by, edge):
    rows = values.shape[0]
    moved = pltpu.roll(values, by % rows, 0)
    return jnp.where(iota(values.shape, 0) % WB == edge, 0.0, moved)


def copy_matrix(e_ref):
    for m in range(BLOCKS):
        source = iota((256, 128), 0)
        lane = iota((256, 128), 1)
        shift, inner = lane // 32, lane % 32
        column, ref_row = 6 * m - 2 + inner // 2, inner % 2
        used = (inner < 20) & (column >= 0) & (column < WA) & (shift < 3)
        hit = used & (source == shift * NA + ref_row * WA + column)
        e_ref[:, 128 * m : 128 * m + 128] = jnp.where(hit, 1.0, 0.0).astype(BF16)


def unit_slices(values, unit, plane, rows):
    values = values.astype(F32)
    scale = lax.rsqrt(jnp.sum(values * values, axis=1, keepdims=True) + EPS_NORM)
    normed = values * scale
    mine = jnp.where(plane == 0, normed[:, 0:HALF], normed[:, HALF : 2 * HALF])
    for s in range(32):
        g, t = s // 4, s % 4
        at = 8 * s
        unit[at // rows, at % rows : at % rows + 8, :] = mine[8 * g : 8 * g + 8, 128 * t : 128 * t + 128].astype(BF16)


def squares_of(feats, out_ref):
    values = feats.astype(F32)
    sums = jnp.sum(values * values, axis=1, keepdims=True)
    for t in range(4):
        wide = jnp.broadcast_to(sums[128 * t : 128 * t + 128], (128, 128))
        out_ref[t : t + 1, :] = jnp.transpose(wide)[0:1, :]


def kernel(
    sizes, owner_hbm, valid_hbm, bf_hbm, bm_hbm, bl_hbm, q_hbm, t_hbm, wf_hbm, wm_hbm, wl_hbm,
    out_ref,
    owner_ref, valid_ref, bf_ref, bm_ref, bl_ref, q_ref, t_ref, wf_ref, wm_ref, wl_ref, unit, recv_a, cand, recv_b, piece, gath, sq_own, sq_oth, part, part_oth,
    tmp, spread, w1, w2, w3, e_ref, vbuf, xbuf, h1, h2, loads, sems,
):
    group, depth, inner, rows = sizes
    me = lax.axis_index("pair")
    plane = lax.axis_index("trow")
    z = lax.rem(me // inner, depth)
    g = (me // (inner * depth)) * inner + lax.rem(me, inner)

    def at(g_of, z_of):
        return ((g_of // inner) * depth + z_of) * inner + lax.rem(g_of, inner)

    cores, columns = min(2, inner), max(1, inner // 2)
    layers = group // inner
    core, x, layer = lax.rem(g, cores), lax.rem(g // cores, columns), g // inner
    steps = [(dy, dx, dc) for dy in range(layers) for dx in range(columns) for dc in range(cores)]
    steps = sorted(steps, key=lambda s: (-s[0] - min(s[1], columns - s[1]), -s[2]))[:-1]
    members = [
        (lax.rem(layer + dy, layers) * columns + lax.rem(x + dx, columns)) * cores + lax.rem(core + dc, cores)
        for dy, dx, dc in steps
    ]
    others = [
        lax.rem(z + o, depth) for o in sorted(range(1, depth), key=lambda o: -min(o, depth - o))
    ]

    barrier = pltpu.get_barrier_semaphore()

    def greet(pair, trow):
        pl.semaphore_signal(barrier, inc=1, device_id=(pair, trow), device_id_type=MESH)

    for other in others:
        greet(at(g, other), plane)
    for member in members:
        greet(at(member, z), plane)
    greet(me, 1 - plane)

    local = [
        pltpu.make_async_copy(src, dst, loads.at[i])
        for i, (src, dst) in enumerate(
            (
                (q_hbm.at[0], q_ref),
                (wf_hbm, wf_ref),
                (wl_hbm, wl_ref),
                (wm_hbm, wm_ref),
                (t_hbm.at[0], t_ref),
                (owner_hbm, owner_ref),
                (valid_hbm, valid_ref),
                (bf_hbm, bf_ref),
                (bm_hbm, bm_ref),
                (bl_hbm, bl_ref),
            )
        )
    ]
    for copy in local:
        copy.start()
    copy_matrix(e_ref)
    local[0].wait()
    unit_slices(q_ref[...], unit, plane, rows)
    for copy in local[1:4]:
        copy.wait()
    prepare(wf_ref, wm_ref, wl_ref, tmp, spread, w1, w2, w3)
    for copy in local[4:]:
        copy.wait()
    squares_of(t_ref[...], sq_own)

    pl.semaphore_wait(barrier, (depth - 1) + (group - 1) + 1)

    def send(src, dst, k, pair, trow):
        copy = pltpu.make_async_remote_copy(
            src_ref=src,
            dst_ref=dst,
            send_sem=sems.at[2 * k],
            recv_sem=sems.at[2 * k + 1],
            device_id=(pair, trow),
            device_id_type=MESH,
        )
        copy.start()
        return copy

    def wait(ref, k):
        pltpu.make_async_copy(ref, ref, sems.at[k]).wait()

    owner = owner_ref[0]
    owner_g = (owner // (inner * depth)) * inner + lax.rem(owner, inner)
    owner_z = lax.rem(owner // inner, depth)

    for member in members:
        send(unit.at[member], recv_a.at[g], 0, at(member, z), plane)
    squares = send(sq_own, sq_oth, 3, me, 1 - plane)
    recv_a[g] = unit[g]
    if group > 1:
        wait(recv_a.at[pl.ds(0, group - 1)], 1)
    chosen = recv_a[owner_g]
    cand[...] = chosen
    recv_b[z] = chosen

    for other in others:
        send(cand, recv_b.at[z], 1, at(g, other), plane)
    wait(recv_b.at[pl.ds(0, depth - 1)], 3)
    chosen = recv_b[owner_z]
    piece[...] = chosen
    gath[g] = chosen

    for member in members:
        send(piece, gath.at[g], 2, at(member, z), plane)
    if group > 1:
        wait(gath.at[pl.ds(0, group - 1)], 5)
    lines = []
    for line in range(8):
        tiles = []
        for t in range(4):
            first = 8 * (4 * line + t)
            tiles.append(gath[first // rows, first % rows : first % rows + 8, :].astype(F32))
        lines.append(jnp.concatenate(tiles, axis=1))
    window = jnp.concatenate(lines, axis=0).astype(BF16)

    blank = jnp.zeros((NA, HALF), BF16)
    partial = []
    for c in range(CHUNKS):
        first = c * (256 // CHUNKS)
        last = first + 256 // CHUNKS
        part[first:last] = nt(t_ref[first:last, :], jnp.concatenate([window, blank], axis=0)) + nt(
            t_ref[256 + first : 256 + last, :], jnp.concatenate([blank, window], axis=0)
        )
        partial.append(send(part.at[pl.ds(first, 256 // CHUNKS)], part_oth.at[pl.ds(first, 256 // CHUNKS)], 4 + c, me, 1 - plane))

    b1 = bias_row(bf_ref, 256)
    b2 = bias_row(bm_ref, 32 * STEP)
    squares.wait()
    columns = []
    for t in range(4):
        total = sq_own[t : t + 1, :] + sq_oth[t : t + 1, :]
        columns.append(jnp.transpose(jnp.broadcast_to(total, (128, 128))))
    inverse = lax.rsqrt(jnp.concatenate(columns, axis=0) + EPS_NORM)
    live = iota((NB, 128), 0) // WB < valid_ref[0]

    for copy in partial:
        copy.wait()
    both = part[...] + part_oth[...]
    swapped = pltpu.roll(both, 64, 1)
    low = iota((256, 128), 1) < 64
    raw = jnp.concatenate([jnp.where(low, both, swapped), jnp.where(low, swapped, both)], axis=0)
    corr = jnp.where(live, math.sqrt(1024) * raw * inverse, 0.0)
    magnitude = jnp.abs(corr)
    peak_query = jnp.max(magnitude, axis=1, keepdims=True)
    peak_target = jnp.max(magnitude, axis=0, keepdims=True)
    volume = corr * (corr * (1.0 / (peak_query + EPS_PEAK))) * (corr * (1.0 / (peak_target + EPS_PEAK)))
    vbuf[0:WB, :] = jnp.zeros((WB, 256), BF16)
    vbuf[WB + NB : 2 * WB + NB, :] = jnp.zeros((WB, 256), BF16)
    low = iota((NB, 128), 1) < 64
    vbuf[WB : WB + NB, 0:128] = jnp.where(low, shifted(volume, 1, 0), volume).astype(BF16)
    vbuf[WB : WB + NB, 128:256] = shifted(volume, -1, WB - 1).astype(BF16)
    start = pl.multiple_of(plane * (6 * WB), 6 * WB)
    xbuf[...] = nn(vbuf[pl.ds(start, 12 * WB), :], e_ref[...]).astype(BF16)

    pad = pl.multiple_of((1 - plane) * WB, WB)

    lane = iota((10 * WB, 256), 1)
    for m in range(BLOCKS):
        acc = nn(xbuf[0 : 10 * WB, 128 * m : 128 * m + 128], w1[0])
        for k in (1, 2):
            acc = acc + nn(xbuf[WB * k : WB * k + 10 * WB, 128 * m : 128 * m + 128], w1[k])
        hidden = jnp.maximum(acc + b1, 0.0)
        if m == 0:
            hidden = jnp.where(lane < 32, 0.0, hidden)
        if m == BLOCKS - 1:
            hidden = jnp.where(lane >= 32 * (WA - 6 * m + 1), 0.0, hidden)
        zero = jnp.zeros((WB, 256), BF16)
        edge = pl.multiple_of(plane * (10 * WB), WB)
        for l in range(3):
            h1[m, l, pl.ds(edge, WB), :] = zero
        h1[m, 0, pl.ds(pad, 10 * WB), :] = shifted(hidden, 1, 0).astype(BF16)
        h1[m, 1, pl.ds(pad, 10 * WB), :] = hidden.astype(BF16)
        h1[m, 2, pl.ds(pad, 10 * WB), :] = shifted(hidden, -1, WB - 1).astype(BF16)

    edge = pl.multiple_of(plane * (9 * WB), WB)
    for m in range(BLOCKS):
        acc = jnp.zeros((9 * WB, 256), F32)
        for k in range(3):
            for l in range(3):
                acc = acc + nt(h1[m, l, WB * k : WB * k + 9 * WB, :], w2[3 * k + l])
        hidden = jnp.maximum(acc + b2, 0.0)
        h2[pl.ds(edge, WB), 256 * m : 256 * m + 256] = jnp.zeros((WB, 256), BF16)
        h2[pl.ds(pad, 9 * WB), 256 * m : 256 * m + 256] = hidden.astype(BF16)

    acc = nt(w3[0], h2[0 : 8 * WB, :])
    for k in (1, 2):
        acc = acc + nt(w3[k], h2[WB * k : WB * k + 8 * WB, :])
    column = iota((NA, 8 * WB), 1) % WB
    result = acc[NA : 2 * NA]
    result = result + jnp.where(column == 0, 0.0, pltpu.roll(acc[0:NA], 1, 1))
    result = result + jnp.where(column == WB - 1, 0.0, pltpu.roll(acc[2 * NA : 3 * NA], 8 * WB - 1, 1))
    result = result + bl_ref[0]
    row = plane * 8 + iota((NA, 8 * WB), 1) // WB
    out_ref[0] = jnp.where(row < valid_ref[0], result, 0.0)

    if group > 1:
        wait(recv_a.at[pl.ds(0, group - 1)], 0)
        wait(gath.at[pl.ds(0, group - 1)], 4)
    wait(recv_b.at[pl.ds(0, depth - 1)], 2)


def layout_of(n):
    inner = min(8, max(1, n // 2))
    depth = min(8, n // inner)
    group = n // depth
    return group, depth, inner, 256 // group


def score(owner, valid, b_first, b_middle, b_last, bank, feats, wf, wm, wl, n):
    hbm = pl.BlockSpec(memory_space=pltpu.HBM)
    sizes = layout_of(n)
    group, depth, _, rows = sizes
    return pl.pallas_call(
        functools.partial(kernel, sizes),
        out_shape=pltpu.VMEM((1, NA, 8 * WB), F32),
        in_specs=[hbm] * 10,
        out_specs=pl.BlockSpec(memory_space=pltpu.VMEM),
        scratch_shapes=[
            pltpu.SMEM((1,), jnp.int32),
            pltpu.SMEM((1,), jnp.int32),
            pltpu.SMEM((16,), F32),
            pltpu.SMEM((16,), F32),
            pltpu.SMEM((1,), F32),
            pltpu.VMEM((NA, 2 * HALF), BF16),
            pltpu.VMEM((NB, HALF), BF16),
            pltpu.VMEM((27, 3, 16), BF16),
            pltpu.VMEM((81, 16, 16), BF16),
            pltpu.VMEM((27, 3, 16), BF16),
            pltpu.VMEM((group, rows, 128), BF16),
            pltpu.VMEM((group, rows, 128), BF16),
            pltpu.VMEM((rows, 128), BF16),
            pltpu.VMEM((depth, rows, 128), BF16),
            pltpu.VMEM((rows, 128), BF16),
            pltpu.VMEM((group, rows, 128), BF16),
            pltpu.VMEM((8, 128), F32),
            pltpu.VMEM((8, 128), F32),
            pltpu.VMEM((256, 128), F32),
            pltpu.VMEM((256, 128), F32),
            pltpu.VMEM((27, 8, 128), F32),
            pltpu.VMEM((81 * 16, 128), F32),
            pltpu.VMEM((3, 128, 256), BF16),
            pltpu.VMEM((9, 256, 256), BF16),
            pltpu.VMEM((3, 192, 1536), BF16),
            pltpu.VMEM((256, 768), BF16),
            pltpu.VMEM((NB + 2 * WB, 256), BF16),
            pltpu.VMEM((12 * WB, 768), BF16),
            pltpu.VMEM((BLOCKS, 3, 11 * WB, 256), BF16),
            pltpu.VMEM((10 * WB, 1536), BF16),
            pltpu.SemaphoreType.DMA((10,)),
            pltpu.SemaphoreType.DMA((8 + 2 * CHUNKS,)),
        ],
        compiler_params=pltpu.CompilerParams(
            collective_id=0, has_side_effects=True, vmem_limit_bytes=60 * 1024 * 1024
        ),
        name="pair_scores",
    )(owner, valid, b_first, b_middle, b_last, bank, feats, wf, wm, wl)


def per_device(
    query_bank, ref_owner, target_feat, valid_rows, w_first, b_first, w_middle, b_middle, w_last, b_last
):
    wf = jnp.transpose(w_first, (1, 2, 3, 4, 5, 0)).reshape(27, 3, 16)
    wl = jnp.transpose(w_last, (0, 2, 3, 4, 5, 1)).reshape(27, 3, 16)
    wm = jnp.transpose(w_middle, (2, 3, 4, 5, 0, 1)).reshape(81, 16, 16)
    n = lax.axis_size("pair")
    return score(ref_owner, valid_rows, b_first, b_middle, b_last, query_bank, target_feat, wf, wm, wl, n)


def solution(mesh):
    in_specs = (
        P("pair", None, None),
        P(),
        P("pair", None, "trow"),
        P("pair"),
        P(),
        P(),
        P(),
        P(),
        P(),
        P(),
    )
    out_specs = P("pair", None, "trow")
    return jax.shard_map(
        per_device, mesh=mesh, in_specs=in_specs, out_specs=out_specs, check_vma=False
    )
```

```python
import functools
import math

import jax
import jax.numpy as jnp
from jax import lax
from jax.experimental import pallas as pl
from jax.experimental.pallas import tpu as pltpu
from jax.sharding import PartitionSpec as P

MESH = pl.DeviceIdType.MESH
WB = 32
WA = 32
HB = 16
NB = HB * WB
NA = 64
EPS_NORM = 1e-06
EPS_PEAK = 1e-05
F32 = jnp.float32
BF16 = jnp.bfloat16

BLOCKS = 6
STEP = 6
HALF = 512
CHUNKS = 2


def nt(left, right):
    return lax.dot_general(left, right, (((1,), (1,)), ((), ())), preferred_element_type=F32)


def nn(left, right):
    return lax.dot_general(left, right, (((1,), (0,)), ((), ())), preferred_element_type=F32)


def iota(shape, dim):
    return lax.broadcasted_iota(jnp.int32, shape, dim)


def spread_rows(src_ref, tmp):
    tmp[...] = jnp.zeros_like(tmp)
    for t in range(27):
        tmp[t, 0:3, 0:16] = src_ref[t].astype(F32)
    flat = tmp[...].reshape(216, 128).astype(BF16)
    take = (iota((128, 128), 1) % 16 == iota((128, 128), 0)).astype(F32).astype(BF16)
    return nn(flat, take)


def bias_row(b_ref, used):
    lane = iota((1, 256), 1)
    row = jnp.zeros((1, 256), F32)
    for o in range(16):
        row = jnp.where(lane % 16 == o, b_ref[o], row)
    return jnp.where(lane < used, row, 0.0)


def prepare(wf_ref, wm_ref, wl_ref, tmp, spread, w1, w2, w3):
    spread[0:216, :] = spread_rows(wf_ref, tmp)
    row = iota((32, 128), 0)
    lane = iota((32, 128), 1)
    for tile in range(2):
        j_of = row // 2 - (tile * 4 + lane // 32)
        i_of = row % 2 - (lane // 16) % 2 + 1
        for k in range(3):
            for l in range(4):
                block = jnp.zeros((32, 128), F32)
                if l < 3:
                    for i in range(3):
                        for j in range(3):
                            t = (i * 3 + j) * 3 + k
                            value = spread[8 * t + l : 8 * t + l + 1, :]
                            block = jnp.where((j_of == j) & (i_of == i), value, block)
                w1[k, 32 * l : 32 * l + 32, 128 * tile : 128 * tile + 128] = block.astype(BF16)

    spread[0:216, :] = spread_rows(wl_ref, tmp)
    row = iota((16, 128), 0)
    lane = iota((16, 128), 1)
    i_of = (lane // 16) % 2 - row // 8 + 1
    for tile in range(2):
        q_of = tile * 4 + lane // 32
        j_of = jnp.where(q_of < STEP, q_of - row % 8 + 2, -1)
        for k in range(3):
            for l in range(3):
                block = jnp.zeros((16, 128), F32)
                for i in range(3):
                    for j in range(3):
                        t = (i * 3 + j) * 3 + k
                        value = spread[8 * t + l : 8 * t + l + 1, :]
                        block = jnp.where((j_of == j) & (i_of == i), value, block)
                at = 16 * (3 * k + l)
                w3[at : at + 16, 128 * tile : 128 * tile + 128] = block.astype(BF16)

    take = (iota((16, 128), 1) % 16 == iota((16, 128), 0)).astype(F32).astype(BF16)
    spread[...] = nn(wm_ref[...].reshape(81 * 16, 16), take)
    odd = (iota((16, 128), 1) // 16) % 2 == 1
    p_of = iota((16, 128), 1) // 32
    for k in range(3):
        for l in range(3):
            w2[3 * k + l, 192:256, :] = jnp.zeros((64, 256), BF16)
            for ra in range(2):
                values = []
                for j in range(3):
                    t0 = (((1 - ra) * 3 + j) * 3 + k) * 3 + l
                    t1 = (((2 - ra) * 3 + j) * 3 + k) * 3 + l
                    values.append(
                        jnp.where(odd, spread[16 * t1 : 16 * t1 + 16, :], spread[16 * t0 : 16 * t0 + 16, :])
                    )
                for q in range(STEP):
                    for tile in range(2):
                        block = jnp.zeros((16, 128), F32)
                        for j in range(3):
                            block = jnp.where(p_of == q + j - 4 * tile, values[j], block)
                        at = 32 * q + 16 * ra
                        w2[3 * k + l, at : at + 16, 128 * tile : 128 * tile + 128] = block.astype(BF16)


def shifted(values, by, edge):
    rows = values.shape[0]
    moved = pltpu.roll(values, by % rows, 0)
    return jnp.where(iota(values.shape, 0) % WB == edge, 0.0, moved)


def copy_matrix(e_ref):
    for m in range(BLOCKS):
        source = iota((256, 128), 0)
        lane = iota((256, 128), 1)
        shift, inner = lane // 32, lane % 32
        column, ref_row = 6 * m - 2 + inner // 2, inner % 2
        used = (inner < 20) & (column >= 0) & (column < WA) & (shift < 3)
        hit = used & (source == shift * NA + ref_row * WA + column)
        e_ref[:, 128 * m : 128 * m + 128] = jnp.where(hit, 1.0, 0.0).astype(BF16)


def unit_slices(values, unit, plane, rows):
    values = values.astype(F32)
    scale = lax.rsqrt(jnp.sum(values * values, axis=1, keepdims=True) + EPS_NORM)
    normed = values * scale
    mine = jnp.where(plane == 0, normed[:, 0:HALF], normed[:, HALF : 2 * HALF])
    for s in range(32):
        g, t = s // 4, s % 4
        at = 8 * s
        unit[at // rows, at % rows : at % rows + 8, :] = mine[8 * g : 8 * g + 8, 128 * t : 128 * t + 128].astype(BF16)


def squares_of(feats, out_ref):
    values = feats.astype(F32)
    sums = jnp.sum(values * values, axis=1, keepdims=True)
    for t in range(4):
        wide = jnp.broadcast_to(sums[128 * t : 128 * t + 128], (128, 128))
        out_ref[t : t + 1, :] = jnp.transpose(wide)[0:1, :]


def kernel(
    sizes, owner_hbm, valid_hbm, bf_hbm, bm_hbm, bl_hbm, q_hbm, t_hbm, wf_hbm, wm_hbm, wl_hbm,
    out_ref,
    owner_ref, valid_ref, bf_ref, bm_ref, bl_ref, q_ref, t_ref, wf_ref, wm_ref, wl_ref, unit, recv_a, cand, recv_b, piece, gath, sq_own, sq_oth, part, part_oth,
    tmp, spread, w1, w2, w3, e_ref, vbuf, xbuf, h1, h2, total, loads, sems,
):
    group, depth, inner, rows = sizes
    me = lax.axis_index("pair")
    plane = lax.axis_index("trow")
    z = lax.rem(me // inner, depth)
    g = (me // (inner * depth)) * inner + lax.rem(me, inner)

    def at(g_of, z_of):
        return ((g_of // inner) * depth + z_of) * inner + lax.rem(g_of, inner)

    cores, columns = min(2, inner), max(1, inner // 2)
    layers = group // inner
    core, x, layer = lax.rem(g, cores), lax.rem(g // cores, columns), g // inner
    steps = [(dy, dx, dc) for dy in range(layers) for dx in range(columns) for dc in range(cores)]
    steps = sorted(steps, key=lambda s: (-s[0] - min(s[1], columns - s[1]), -s[2]))[:-1]
    members = [
        (lax.rem(layer + dy, layers) * columns + lax.rem(x + dx, columns)) * cores + lax.rem(core + dc, cores)
        for dy, dx, dc in steps
    ]
    others = [
        lax.rem(z + o, depth) for o in sorted(range(1, depth), key=lambda o: -min(o, depth - o))
    ]

    barrier = pltpu.get_barrier_semaphore()

    def greet(pair, trow):
        pl.semaphore_signal(barrier, inc=1, device_id=(pair, trow), device_id_type=MESH)

    for other in others:
        greet(at(g, other), plane)
    for member in members:
        greet(at(member, z), plane)
    greet(me, 1 - plane)

    local = [
        pltpu.make_async_copy(src, dst, loads.at[i])
        for i, (src, dst) in enumerate(
            (
                (q_hbm.at[0], q_ref),
                (wf_hbm, wf_ref),
                (wl_hbm, wl_ref),
                (wm_hbm, wm_ref),
                (t_hbm.at[0], t_ref),
                (owner_hbm, owner_ref),
                (valid_hbm, valid_ref),
                (bf_hbm, bf_ref),
                (bm_hbm, bm_ref),
                (bl_hbm, bl_ref),
            )
        )
    ]
    for copy in local:
        copy.start()
    copy_matrix(e_ref)
    local[0].wait()
    unit_slices(q_ref[...], unit, plane, rows)
    for copy in local[1:4]:
        copy.wait()
    prepare(wf_ref, wm_ref, wl_ref, tmp, spread, w1, w2, w3)
    for copy in local[4:]:
        copy.wait()
    squares_of(t_ref[...], sq_own)

    pl.semaphore_wait(barrier, (depth - 1) + (group - 1) + 1)

    def send(src, dst, k, pair, trow):
        copy = pltpu.make_async_remote_copy(
            src_ref=src,
            dst_ref=dst,
            send_sem=sems.at[2 * k],
            recv_sem=sems.at[2 * k + 1],
            device_id=(pair, trow),
            device_id_type=MESH,
        )
        copy.start()
        return copy

    def wait(ref, k):
        pltpu.make_async_copy(ref, ref, sems.at[k]).wait()

    owner = owner_ref[0]
    owner_g = (owner // (inner * depth)) * inner + lax.rem(owner, inner)
    owner_z = lax.rem(owner // inner, depth)

    for member in members:
        send(unit.at[member], recv_a.at[g], 0, at(member, z), plane)
    squares = send(sq_own, sq_oth, 3, me, 1 - plane)
    recv_a[g] = unit[g]
    if group > 1:
        wait(recv_a.at[pl.ds(0, group - 1)], 1)
    chosen = recv_a[owner_g]
    cand[...] = chosen
    recv_b[z] = chosen

    for other in others:
        send(cand, recv_b.at[z], 1, at(g, other), plane)
    wait(recv_b.at[pl.ds(0, depth - 1)], 3)
    chosen = recv_b[owner_z]
    piece[...] = chosen
    gath[g] = chosen

    for member in members:
        send(piece, gath.at[g], 2, at(member, z), plane)
    if group > 1:
        wait(gath.at[pl.ds(0, group - 1)], 5)
    lines = []
    for line in range(8):
        tiles = []
        for t in range(4):
            first = 8 * (4 * line + t)
            tiles.append(gath[first // rows, first % rows : first % rows + 8, :].astype(F32))
        lines.append(jnp.concatenate(tiles, axis=1))
    window = jnp.concatenate(lines, axis=0).astype(BF16)

    blank = jnp.zeros((NA, HALF), BF16)
    partial = []
    for c in range(CHUNKS):
        first = c * (256 // CHUNKS)
        last = first + 256 // CHUNKS
        part[first:last] = nt(t_ref[first:last, :], jnp.concatenate([window, blank], axis=0)) + nt(
            t_ref[256 + first : 256 + last, :], jnp.concatenate([blank, window], axis=0)
        )
        partial.append(send(part.at[pl.ds(first, 256 // CHUNKS)], part_oth.at[pl.ds(first, 256 // CHUNKS)], 4 + c, me, 1 - plane))

    b1 = bias_row(bf_ref, 256)
    b2 = bias_row(bm_ref, 32 * STEP)
    squares.wait()
    columns = []
    for t in range(4):
        both = sq_own[t : t + 1, :] + sq_oth[t : t + 1, :]
        columns.append(jnp.transpose(jnp.broadcast_to(both, (128, 128))))
    inverse = lax.rsqrt(jnp.concatenate(columns, axis=0) + EPS_NORM)
    live = iota((NB, 128), 0) // WB < valid_ref[0]

    for copy in partial:
        copy.wait()
    both = part[...] + part_oth[...]
    swapped = pltpu.roll(both, 64, 1)
    low = iota((256, 128), 1) < 64
    raw = jnp.concatenate([jnp.where(low, both, swapped), jnp.where(low, swapped, both)], axis=0)
    corr = jnp.where(live, math.sqrt(1024) * raw * inverse, 0.0)
    magnitude = jnp.abs(corr)
    peak_query = jnp.max(magnitude, axis=1, keepdims=True)
    peak_target = jnp.max(magnitude, axis=0, keepdims=True)
    volume = corr * (corr * (1.0 / (peak_query + EPS_PEAK))) * (corr * (1.0 / (peak_target + EPS_PEAK)))
    vbuf[0:WB, :] = jnp.zeros((WB, 256), BF16)
    vbuf[WB + NB : 2 * WB + NB, :] = jnp.zeros((WB, 256), BF16)
    low = iota((NB, 128), 1) < 64
    vbuf[WB : WB + NB, 0:128] = jnp.where(low, shifted(volume, 1, 0), volume).astype(BF16)
    vbuf[WB : WB + NB, 128:256] = shifted(volume, -1, WB - 1).astype(BF16)
    start = pl.multiple_of(plane * (6 * WB), 6 * WB)
    xbuf[...] = nn(vbuf[pl.ds(start, 12 * WB), :], e_ref[...]).astype(BF16)

    pad = pl.multiple_of((1 - plane) * WB, WB)

    lane = iota((10 * WB, 256), 1)
    for m in range(BLOCKS):
        acc = nn(xbuf[0 : 10 * WB, 128 * m : 128 * m + 128], w1[0])
        for k in (1, 2):
            acc = acc + nn(xbuf[WB * k : WB * k + 10 * WB, 128 * m : 128 * m + 128], w1[k])
        hidden = jnp.maximum(acc + b1, 0.0)
        if m == 0:
            hidden = jnp.where(lane < 32, 0.0, hidden)
        if m == BLOCKS - 1:
            hidden = jnp.where(lane >= 32 * (WA - 6 * m + 1), 0.0, hidden)
        zero = jnp.zeros((WB, 256), BF16)
        edge = pl.multiple_of(plane * (10 * WB), WB)
        for l in range(3):
            h1[m, l, pl.ds(edge, WB), :] = zero
        h1[m, 0, pl.ds(pad, 10 * WB), :] = shifted(hidden, 1, 0).astype(BF16)
        h1[m, 1, pl.ds(pad, 10 * WB), :] = hidden.astype(BF16)
        h1[m, 2, pl.ds(pad, 10 * WB), :] = shifted(hidden, -1, WB - 1).astype(BF16)

    edge = pl.multiple_of(plane * (9 * WB), WB)
    for m in range(BLOCKS):
        acc = jnp.zeros((9 * WB, 256), F32)
        for k in range(3):
            for l in range(3):
                acc = acc + nt(h1[m, l, WB * k : WB * k + 9 * WB, :], w2[3 * k + l])
        hidden = jnp.maximum(acc + b2, 0.0)
        if m == BLOCKS - 1:
            hidden = jnp.where(iota((9 * WB, 256), 1) < 32 * (WA - STEP * m), hidden, 0.0)
        h2[pl.ds(edge, WB), 256 * m : 256 * m + 256] = jnp.zeros((WB, 256), BF16)
        h2[pl.ds(pad, 9 * WB), 256 * m : 256 * m + 256] = hidden.astype(BF16)

    column = iota((16, 8 * WB), 1) % WB
    total[...] = jnp.zeros_like(total)
    for m in range(BLOCKS):
        acc = nt(w3[...], h2[:, 256 * m : 256 * m + 256])
        sums = []
        for l in range(3):
            terms = [acc[16 * (3 * k + l) : 16 * (3 * k + l) + 16] for k in range(3)]
            moved = [terms[0]] + [pltpu.roll(terms[k], 12 * WB - WB * k, 1) for k in (1, 2)]
            sums.append(moved[0][:, 0 : 8 * WB] + moved[1][:, 0 : 8 * WB] + moved[2][:, 0 : 8 * WB])
        block = sums[1]
        block = block + jnp.where(column == 0, 0.0, pltpu.roll(sums[0], 1, 1))
        block = block + jnp.where(column == WB - 1, 0.0, pltpu.roll(sums[2], 8 * WB - 1, 1))
        for ra in range(2):
            total[ra, STEP * m : STEP * m + 8, :] += block[8 * ra : 8 * ra + 8]
    row = plane * 8 + iota((WA, 8 * WB), 1) // WB
    for ra in range(2):
        result = total[ra, 1 : 1 + WA, :] + bl_ref[0]
        out_ref[0, WA * ra : WA * ra + WA, :] = jnp.where(row < valid_ref[0], result, 0.0)

    if group > 1:
        wait(recv_a.at[pl.ds(0, group - 1)], 0)
        wait(gath.at[pl.ds(0, group - 1)], 4)
    wait(recv_b.at[pl.ds(0, depth - 1)], 2)


def layout_of(n):
    inner = min(8, max(1, n // 2))
    depth = min(8, n // inner)
    group = n // depth
    return group, depth, inner, 256 // group


def score(owner, valid, b_first, b_middle, b_last, bank, feats, wf, wm, wl, n):
    hbm = pl.BlockSpec(memory_space=pltpu.HBM)
    sizes = layout_of(n)
    group, depth, _, rows = sizes
    return pl.pallas_call(
        functools.partial(kernel, sizes),
        out_shape=pltpu.VMEM((1, NA, 8 * WB), F32),
        in_specs=[hbm] * 10,
        out_specs=pl.BlockSpec(memory_space=pltpu.VMEM),
        scratch_shapes=[
            pltpu.SMEM((1,), jnp.int32),
            pltpu.SMEM((1,), jnp.int32),
            pltpu.SMEM((16,), F32),
            pltpu.SMEM((16,), F32),
            pltpu.SMEM((1,), F32),
            pltpu.VMEM((NA, 2 * HALF), BF16),
            pltpu.VMEM((NB, HALF), BF16),
            pltpu.VMEM((27, 3, 16), BF16),
            pltpu.VMEM((81, 16, 16), BF16),
            pltpu.VMEM((27, 3, 16), BF16),
            pltpu.VMEM((group, rows, 128), BF16),
            pltpu.VMEM((group, rows, 128), BF16),
            pltpu.VMEM((rows, 128), BF16),
            pltpu.VMEM((depth, rows, 128), BF16),
            pltpu.VMEM((rows, 128), BF16),
            pltpu.VMEM((group, rows, 128), BF16),
            pltpu.VMEM((8, 128), F32),
            pltpu.VMEM((8, 128), F32),
            pltpu.VMEM((256, 128), F32),
            pltpu.VMEM((256, 128), F32),
            pltpu.VMEM((27, 8, 128), F32),
            pltpu.VMEM((81 * 16, 128), F32),
            pltpu.VMEM((3, 128, 256), BF16),
            pltpu.VMEM((9, 256, 256), BF16),
            pltpu.VMEM((144, 256), BF16),
            pltpu.VMEM((256, 768), BF16),
            pltpu.VMEM((NB + 2 * WB, 256), BF16),
            pltpu.VMEM((12 * WB, 768), BF16),
            pltpu.VMEM((BLOCKS, 3, 11 * WB, 256), BF16),
            pltpu.VMEM((12 * WB, 1536), BF16),
            pltpu.VMEM((2, 40, 8 * WB), F32),
            pltpu.SemaphoreType.DMA((10,)),
            pltpu.SemaphoreType.DMA((8 + 2 * CHUNKS,)),
        ],
        compiler_params=pltpu.CompilerParams(
            collective_id=0, has_side_effects=True, vmem_limit_bytes=60 * 1024 * 1024
        ),
        name="pair_scores",
    )(owner, valid, b_first, b_middle, b_last, bank, feats, wf, wm, wl)


def per_device(
    query_bank, ref_owner, target_feat, valid_rows, w_first, b_first, w_middle, b_middle, w_last, b_last
):
    wf = jnp.transpose(w_first, (1, 2, 3, 4, 5, 0)).reshape(27, 3, 16)
    wl = jnp.transpose(w_last, (0, 2, 3, 4, 5, 1)).reshape(27, 3, 16)
    wm = jnp.transpose(w_middle, (2, 3, 4, 5, 0, 1)).reshape(81, 16, 16)
    n = lax.axis_size("pair")
    return score(ref_owner, valid_rows, b_first, b_middle, b_last, query_bank, target_feat, wf, wm, wl, n)


def solution(mesh):
    in_specs = (
        P("pair", None, None),
        P(),
        P("pair", None, "trow"),
        P("pair"),
        P(),
        P(),
        P(),
        P(),
        P(),
        P(),
    )
    out_specs = P("pair", None, "trow")
    return jax.shard_map(
        per_device, mesh=mesh, in_specs=in_specs, out_specs=out_specs, check_vma=False
    )
```

```python
import functools
import math

import jax
import jax.numpy as jnp
from jax import lax
from jax.experimental import pallas as pl
from jax.experimental.pallas import tpu as pltpu
from jax.sharding import PartitionSpec as P

MESH = pl.DeviceIdType.MESH
WB = 32
WA = 32
HB = 16
NB = HB * WB
NA = 64
EPS_NORM = 1e-06
EPS_PEAK = 1e-05
F32 = jnp.float32
BF16 = jnp.bfloat16

BLOCKS = 6
STEP = 6
HALF = 512
CHUNKS = 2


def nt(left, right):
    return lax.dot_general(left, right, (((1,), (1,)), ((), ())), preferred_element_type=F32)


def nn(left, right):
    return lax.dot_general(left, right, (((1,), (0,)), ((), ())), preferred_element_type=F32)


def iota(shape, dim):
    return lax.broadcasted_iota(jnp.int32, shape, dim)


def spread_rows(src_ref, tmp):
    tmp[...] = jnp.zeros_like(tmp)
    for t in range(27):
        tmp[t, 0:3, 0:16] = src_ref[t].astype(F32)
    flat = tmp[...].reshape(216, 128).astype(BF16)
    take = (iota((128, 128), 1) % 16 == iota((128, 128), 0)).astype(F32).astype(BF16)
    return nn(flat, take)


def bias_row(b_ref, used):
    lane = iota((1, 256), 1)
    row = jnp.zeros((1, 256), F32)
    for o in range(16):
        row = jnp.where(lane % 16 == o, b_ref[o], row)
    return jnp.where(lane < used, row, 0.0)


def prepare(wf_ref, wm_ref, wl_ref, tmp, spread, w1, w2, w3):
    spread[0:216, :] = spread_rows(wf_ref, tmp)
    row = iota((32, 128), 0)
    lane = iota((32, 128), 1)
    for tile in range(2):
        j_of = row // 2 - (tile * 4 + lane // 32)
        i_of = row % 2 - (lane // 16) % 2 + 1
        for k in range(3):
            for l in range(4):
                block = jnp.zeros((32, 128), F32)
                if l < 3:
                    for i in range(3):
                        for j in range(3):
                            t = (i * 3 + j) * 3 + k
                            value = spread[8 * t + l : 8 * t + l + 1, :]
                            block = jnp.where((j_of == j) & (i_of == i), value, block)
                at = 128 * k + 32 * l
                w1[at : at + 32, 128 * tile : 128 * tile + 128] = block.astype(BF16)

    spread[0:216, :] = spread_rows(wl_ref, tmp)
    row = iota((16, 128), 0)
    lane = iota((16, 128), 1)
    i_of = (lane // 16) % 2 - row // 8 + 1
    for tile in range(2):
        q_of = tile * 4 + lane // 32
        j_of = jnp.where(q_of < STEP, q_of - row % 8 + 2, -1)
        for k in range(3):
            for l in range(3):
                block = jnp.zeros((16, 128), F32)
                for i in range(3):
                    for j in range(3):
                        t = (i * 3 + j) * 3 + k
                        value = spread[8 * t + l : 8 * t + l + 1, :]
                        block = jnp.where((j_of == j) & (i_of == i), value, block)
                at = 16 * (3 * k + l)
                w3[at : at + 16, 128 * tile : 128 * tile + 128] = block.astype(BF16)

    take = (iota((16, 128), 1) % 16 == iota((16, 128), 0)).astype(F32).astype(BF16)
    spread[...] = nn(wm_ref[...].reshape(81 * 16, 16), take)
    odd = (iota((16, 128), 1) // 16) % 2 == 1
    p_of = iota((16, 128), 1) // 32
    for k in range(3):
        for l in range(3):
            w2[3 * k + l, 192:256, :] = jnp.zeros((64, 256), BF16)
            for ra in range(2):
                values = []
                for j in range(3):
                    t0 = (((1 - ra) * 3 + j) * 3 + k) * 3 + l
                    t1 = (((2 - ra) * 3 + j) * 3 + k) * 3 + l
                    values.append(
                        jnp.where(odd, spread[16 * t1 : 16 * t1 + 16, :], spread[16 * t0 : 16 * t0 + 16, :])
                    )
                for q in range(STEP):
                    for tile in range(2):
                        block = jnp.zeros((16, 128), F32)
                        for j in range(3):
                            block = jnp.where(p_of == q + j - 4 * tile, values[j], block)
                        at = 32 * q + 16 * ra
                        w2[3 * k + l, at : at + 16, 128 * tile : 128 * tile + 128] = block.astype(BF16)


def shifted(values, by, edge):
    rows = values.shape[0]
    moved = pltpu.roll(values, by % rows, 0)
    return jnp.where(iota(values.shape, 0) % WB == edge, 0.0, moved)


def copy_matrix(e_ref):
    for m in range(BLOCKS):
        source = iota((256, 128), 0)
        lane = iota((256, 128), 1)
        shift, inner = lane // 32, lane % 32
        column, ref_row = 6 * m - 2 + inner // 2, inner % 2
        used = (inner < 20) & (column >= 0) & (column < WA) & (shift < 3)
        hit = used & (source == shift * NA + ref_row * WA + column)
        e_ref[:, 128 * m : 128 * m + 128] = jnp.where(hit, 1.0, 0.0).astype(BF16)


def unit_slices(values, unit, plane, rows):
    values = values.astype(F32)
    scale = lax.rsqrt(jnp.sum(values * values, axis=1, keepdims=True) + EPS_NORM)
    normed = values * scale
    mine = jnp.where(plane == 0, normed[:, 0:HALF], normed[:, HALF : 2 * HALF])
    for s in range(32):
        g, t = s // 4, s % 4
        at = 8 * s
        unit[at // rows, at % rows : at % rows + 8, :] = mine[8 * g : 8 * g + 8, 128 * t : 128 * t + 128].astype(BF16)


def squares_of(feats, out_ref):
    values = feats.astype(F32)
    sums = jnp.sum(values * values, axis=1, keepdims=True)
    for t in range(4):
        wide = jnp.broadcast_to(sums[128 * t : 128 * t + 128], (128, 128))
        out_ref[t : t + 1, :] = jnp.transpose(wide)[0:1, :]


def kernel(
    sizes, owner_hbm, valid_hbm, bf_hbm, bm_hbm, bl_hbm, q_hbm, t_hbm, wf_hbm, wm_hbm, wl_hbm,
    out_ref,
    owner_ref, valid_ref, bf_ref, bm_ref, bl_ref, q_ref, t_ref, wf_ref, wm_ref, wl_ref, unit, recv_a, cand, recv_b, piece, gath, sq_own, sq_oth, part, part_oth,
    tmp, spread, w1, w2, w3, e_ref, vbuf, xbuf, h1, h2, total, loads, sems,
):
    group, depth, inner, rows = sizes
    me = lax.axis_index("pair")
    plane = lax.axis_index("trow")
    z = lax.rem(me // inner, depth)
    g = (me // (inner * depth)) * inner + lax.rem(me, inner)

    def at(g_of, z_of):
        return ((g_of // inner) * depth + z_of) * inner + lax.rem(g_of, inner)

    cores, columns = min(2, inner), max(1, inner // 2)
    layers = group // inner
    core, x, layer = lax.rem(g, cores), lax.rem(g // cores, columns), g // inner
    steps = [(dy, dx, dc) for dy in range(layers) for dx in range(columns) for dc in range(cores)]
    steps = sorted(steps, key=lambda s: (-s[0] - min(s[1], columns - s[1]), -s[2]))[:-1]
    members = [
        (lax.rem(layer + dy, layers) * columns + lax.rem(x + dx, columns)) * cores + lax.rem(core + dc, cores)
        for dy, dx, dc in steps
    ]
    others = [
        lax.rem(z + o, depth) for o in sorted(range(1, depth), key=lambda o: -min(o, depth - o))
    ]

    barrier = pltpu.get_barrier_semaphore()

    def greet(pair, trow):
        pl.semaphore_signal(barrier, inc=1, device_id=(pair, trow), device_id_type=MESH)

    for other in others:
        greet(at(g, other), plane)
    for member in members:
        greet(at(member, z), plane)
    greet(me, 1 - plane)

    local = [
        pltpu.make_async_copy(src, dst, loads.at[i])
        for i, (src, dst) in enumerate(
            (
                (q_hbm.at[0], q_ref),
                (wf_hbm, wf_ref),
                (wl_hbm, wl_ref),
                (wm_hbm, wm_ref),
                (t_hbm.at[0], t_ref),
                (owner_hbm, owner_ref),
                (valid_hbm, valid_ref),
                (bf_hbm, bf_ref),
                (bm_hbm, bm_ref),
                (bl_hbm, bl_ref),
            )
        )
    ]
    for copy in local:
        copy.start()
    copy_matrix(e_ref)
    local[0].wait()
    unit_slices(q_ref[...], unit, plane, rows)
    for copy in local[1:4]:
        copy.wait()
    prepare(wf_ref, wm_ref, wl_ref, tmp, spread, w1, w2, w3)
    for copy in local[4:]:
        copy.wait()
    squares_of(t_ref[...], sq_own)

    pl.semaphore_wait(barrier, (depth - 1) + (group - 1) + 1)

    def send(src, dst, k, pair, trow):
        copy = pltpu.make_async_remote_copy(
            src_ref=src,
            dst_ref=dst,
            send_sem=sems.at[2 * k],
            recv_sem=sems.at[2 * k + 1],
            device_id=(pair, trow),
            device_id_type=MESH,
        )
        copy.start()
        return copy

    def wait(ref, k):
        pltpu.make_async_copy(ref, ref, sems.at[k]).wait()

    owner = owner_ref[0]
    owner_g = (owner // (inner * depth)) * inner + lax.rem(owner, inner)
    owner_z = lax.rem(owner // inner, depth)

    for member in members:
        send(unit.at[member], recv_a.at[g], 0, at(member, z), plane)
    squares = send(sq_own, sq_oth, 3, me, 1 - plane)
    recv_a[g] = unit[g]
    if group > 1:
        wait(recv_a.at[pl.ds(0, group - 1)], 1)
    chosen = recv_a[owner_g]
    cand[...] = chosen
    recv_b[z] = chosen

    for other in others:
        send(cand, recv_b.at[z], 1, at(g, other), plane)
    wait(recv_b.at[pl.ds(0, depth - 1)], 3)
    chosen = recv_b[owner_z]
    piece[...] = chosen
    gath[g] = chosen

    for member in members:
        send(piece, gath.at[g], 2, at(member, z), plane)
    if group > 1:
        wait(gath.at[pl.ds(0, group - 1)], 5)
    lines = []
    for line in range(8):
        tiles = []
        for t in range(4):
            first = 8 * (4 * line + t)
            tiles.append(gath[first // rows, first % rows : first % rows + 8, :].astype(F32))
        lines.append(jnp.concatenate(tiles, axis=1))
    window = jnp.concatenate(lines, axis=0).astype(BF16)

    blank = jnp.zeros((NA, HALF), BF16)
    partial = []
    for c in range(CHUNKS):
        first = c * (256 // CHUNKS)
        last = first + 256 // CHUNKS
        part[first:last] = nt(t_ref[first:last, :], jnp.concatenate([window, blank], axis=0)) + nt(
            t_ref[256 + first : 256 + last, :], jnp.concatenate([blank, window], axis=0)
        )
        partial.append(send(part.at[pl.ds(first, 256 // CHUNKS)], part_oth.at[pl.ds(first, 256 // CHUNKS)], 4 + c, me, 1 - plane))

    b1 = bias_row(bf_ref, 256)
    b2 = bias_row(bm_ref, 32 * STEP)
    squares.wait()
    columns = []
    for t in range(4):
        both = sq_own[t : t + 1, :] + sq_oth[t : t + 1, :]
        columns.append(jnp.transpose(jnp.broadcast_to(both, (128, 128))))
    inverse = lax.rsqrt(jnp.concatenate(columns, axis=0) + EPS_NORM)
    live = iota((NB, 128), 0) // WB < valid_ref[0]

    for copy in partial:
        copy.wait()
    both = part[...] + part_oth[...]
    swapped = pltpu.roll(both, 64, 1)
    low = iota((256, 128), 1) < 64
    raw = jnp.concatenate([jnp.where(low, both, swapped), jnp.where(low, swapped, both)], axis=0)
    corr = jnp.where(live, math.sqrt(1024) * raw * inverse, 0.0)
    magnitude = jnp.abs(corr)
    peak_query = jnp.max(magnitude, axis=1, keepdims=True)
    peak_target = jnp.max(magnitude, axis=0, keepdims=True)
    volume = corr * (corr * (1.0 / (peak_query + EPS_PEAK))) * (corr * (1.0 / (peak_target + EPS_PEAK)))
    vbuf[0:WB, :] = jnp.zeros((WB, 256), BF16)
    vbuf[WB + NB : 2 * WB + NB, :] = jnp.zeros((WB, 256), BF16)
    low = iota((NB, 128), 1) < 64
    vbuf[WB : WB + NB, 0:128] = jnp.where(low, shifted(volume, 1, 0), volume).astype(BF16)
    vbuf[WB : WB + NB, 128:256] = shifted(volume, -1, WB - 1).astype(BF16)
    start = pl.multiple_of(plane * (6 * WB), 6 * WB)
    xbuf[...] = nn(vbuf[pl.ds(start, 12 * WB), :], e_ref[...]).astype(BF16)

    pad = pl.multiple_of((1 - plane) * WB, WB)

    lane = iota((10 * WB, 256), 1)
    for m in range(BLOCKS):
        taps = [xbuf[WB * k : WB * k + 10 * WB, 128 * m : 128 * m + 128] for k in range(3)]
        acc = nn(jnp.concatenate(taps[0:2], axis=1), w1[0:256, :]) + nn(taps[2], w1[256:384, :])
        hidden = jnp.maximum(acc + b1, 0.0)
        if m == 0:
            hidden = jnp.where(lane < 32, 0.0, hidden)
        if m == BLOCKS - 1:
            hidden = jnp.where(lane >= 32 * (WA - 6 * m + 1), 0.0, hidden)
        zero = jnp.zeros((WB, 256), BF16)
        edge = pl.multiple_of(plane * (10 * WB), WB)
        for l in range(3):
            h1[m, l, pl.ds(edge, WB), :] = zero
        h1[m, 0, pl.ds(pad, 10 * WB), :] = shifted(hidden, 1, 0).astype(BF16)
        h1[m, 1, pl.ds(pad, 10 * WB), :] = hidden.astype(BF16)
        h1[m, 2, pl.ds(pad, 10 * WB), :] = shifted(hidden, -1, WB - 1).astype(BF16)

    edge = pl.multiple_of(plane * (9 * WB), WB)
    for m in range(BLOCKS):
        acc = jnp.zeros((9 * WB, 256), F32)
        for k in range(3):
            for l in range(3):
                acc = acc + nt(h1[m, l, WB * k : WB * k + 9 * WB, :], w2[3 * k + l])
        hidden = jnp.maximum(acc + b2, 0.0)
        if m == BLOCKS - 1:
            hidden = jnp.where(iota((9 * WB, 256), 1) < 32 * (WA - STEP * m), hidden, 0.0)
        h2[pl.ds(edge, WB), 256 * m : 256 * m + 256] = jnp.zeros((WB, 256), BF16)
        h2[pl.ds(pad, 9 * WB), 256 * m : 256 * m + 256] = hidden.astype(BF16)

    column = iota((16, 8 * WB), 1) % WB
    total[...] = jnp.zeros_like(total)
    for m in range(BLOCKS):
        acc = nt(w3[...], h2[:, 256 * m : 256 * m + 256])
        sums = []
        for l in range(3):
            terms = [acc[16 * (3 * k + l) : 16 * (3 * k + l) + 16] for k in range(3)]
            moved = [terms[0]] + [pltpu.roll(terms[k], 12 * WB - WB * k, 1) for k in (1, 2)]
            sums.append(moved[0][:, 0 : 8 * WB] + moved[1][:, 0 : 8 * WB] + moved[2][:, 0 : 8 * WB])
        block = sums[1]
        block = block + jnp.where(column == 0, 0.0, pltpu.roll(sums[0], 1, 1))
        block = block + jnp.where(column == WB - 1, 0.0, pltpu.roll(sums[2], 8 * WB - 1, 1))
        for ra in range(2):
            total[ra, STEP * m : STEP * m + 8, :] += block[8 * ra : 8 * ra + 8]
    row = plane * 8 + iota((WA, 8 * WB), 1) // WB
    for ra in range(2):
        result = total[ra, 1 : 1 + WA, :] + bl_ref[0]
        out_ref[0, WA * ra : WA * ra + WA, :] = jnp.where(row < valid_ref[0], result, 0.0)

    if group > 1:
        wait(recv_a.at[pl.ds(0, group - 1)], 0)
        wait(gath.at[pl.ds(0, group - 1)], 4)
    wait(recv_b.at[pl.ds(0, depth - 1)], 2)


def layout_of(n):
    inner = min(8, max(1, n // 2))
    depth = min(8, n // inner)
    group = n // depth
    return group, depth, inner, 256 // group


def score(owner, valid, b_first, b_middle, b_last, bank, feats, wf, wm, wl, n):
    hbm = pl.BlockSpec(memory_space=pltpu.HBM)
    sizes = layout_of(n)
    group, depth, _, rows = sizes
    return pl.pallas_call(
        functools.partial(kernel, sizes),
        out_shape=pltpu.VMEM((1, NA, 8 * WB), F32),
        in_specs=[hbm] * 10,
        out_specs=pl.BlockSpec(memory_space=pltpu.VMEM),
        scratch_shapes=[
            pltpu.SMEM((1,), jnp.int32),
            pltpu.SMEM((1,), jnp.int32),
            pltpu.SMEM((16,), F32),
            pltpu.SMEM((16,), F32),
            pltpu.SMEM((1,), F32),
            pltpu.VMEM((NA, 2 * HALF), BF16),
            pltpu.VMEM((NB, HALF), BF16),
            pltpu.VMEM((27, 3, 16), BF16),
            pltpu.VMEM((81, 16, 16), BF16),
            pltpu.VMEM((27, 3, 16), BF16),
            pltpu.VMEM((group, rows, 128), BF16),
            pltpu.VMEM((group, rows, 128), BF16),
            pltpu.VMEM((rows, 128), BF16),
            pltpu.VMEM((depth, rows, 128), BF16),
            pltpu.VMEM((rows, 128), BF16),
            pltpu.VMEM((group, rows, 128), BF16),
            pltpu.VMEM((8, 128), F32),
            pltpu.VMEM((8, 128), F32),
            pltpu.VMEM((256, 128), F32),
            pltpu.VMEM((256, 128), F32),
            pltpu.VMEM((27, 8, 128), F32),
            pltpu.VMEM((81 * 16, 128), F32),
            pltpu.VMEM((384, 256), BF16),
            pltpu.VMEM((9, 256, 256), BF16),
            pltpu.VMEM((144, 256), BF16),
            pltpu.VMEM((256, 768), BF16),
            pltpu.VMEM((NB + 2 * WB, 256), BF16),
            pltpu.VMEM((12 * WB, 768), BF16),
            pltpu.VMEM((BLOCKS, 3, 11 * WB, 256), BF16),
            pltpu.VMEM((12 * WB, 1536), BF16),
            pltpu.VMEM((2, 40, 8 * WB), F32),
            pltpu.SemaphoreType.DMA((10,)),
            pltpu.SemaphoreType.DMA((8 + 2 * CHUNKS,)),
        ],
        compiler_params=pltpu.CompilerParams(
            collective_id=0, has_side_effects=True, vmem_limit_bytes=60 * 1024 * 1024
        ),
        name="pair_scores",
    )(owner, valid, b_first, b_middle, b_last, bank, feats, wf, wm, wl)


def per_device(
    query_bank, ref_owner, target_feat, valid_rows, w_first, b_first, w_middle, b_middle, w_last, b_last
):
    wf = jnp.transpose(w_first, (1, 2, 3, 4, 5, 0)).reshape(27, 3, 16)
    wl = jnp.transpose(w_last, (0, 2, 3, 4, 5, 1)).reshape(27, 3, 16)
    wm = jnp.transpose(w_middle, (2, 3, 4, 5, 0, 1)).reshape(81, 16, 16)
    n = lax.axis_size("pair")
    return score(ref_owner, valid_rows, b_first, b_middle, b_last, query_bank, target_feat, wf, wm, wl, n)


def solution(mesh):
    in_specs = (
        P("pair", None, None),
        P(),
        P("pair", None, "trow"),
        P("pair"),
        P(),
        P(),
        P(),
        P(),
        P(),
        P(),
    )
    out_specs = P("pair", None, "trow")
    return jax.shard_map(
        per_device, mesh=mesh, in_specs=in_specs, out_specs=out_specs, check_vma=False
    )
```

```python
import functools
import math

import jax
import jax.numpy as jnp
from jax import lax
from jax.experimental import pallas as pl
from jax.experimental.pallas import tpu as pltpu
from jax.sharding import PartitionSpec as P

MESH = pl.DeviceIdType.MESH
WB = 32
WA = 32
HB = 16
NB = HB * WB
NA = 64
EPS_NORM = 1e-06
EPS_PEAK = 1e-05
F32 = jnp.float32
BF16 = jnp.bfloat16

BLOCKS = 6
STEP = 6
HALF = 512
CHUNKS = 2


def nt(left, right):
    return lax.dot_general(left, right, (((1,), (1,)), ((), ())), preferred_element_type=F32)


def nn(left, right):
    return lax.dot_general(left, right, (((1,), (0,)), ((), ())), preferred_element_type=F32)


def iota(shape, dim):
    return lax.broadcasted_iota(jnp.int32, shape, dim)


def spread_rows(src_ref, tmp):
    tmp[...] = jnp.zeros_like(tmp)
    for t in range(27):
        tmp[t, 0:3, 0:16] = src_ref[t].astype(F32)
    flat = tmp[...].reshape(216, 128).astype(BF16)
    take = (iota((128, 128), 1) % 16 == iota((128, 128), 0)).astype(F32).astype(BF16)
    return nn(flat, take)


def bias_row(b_ref, used):
    lane = iota((1, 256), 1)
    row = jnp.zeros((1, 256), F32)
    for o in range(16):
        row = jnp.where(lane % 16 == o, b_ref[o], row)
    return jnp.where(lane < used, row, 0.0)


def prepare(wf_ref, wm_ref, wl_ref, tmp, spread, w1, w2, w3):
    spread[0:216, :] = spread_rows(wf_ref, tmp)
    row = iota((32, 128), 0)
    lane = iota((32, 128), 1)
    for tile in range(2):
        j_of = row // 2 - (tile * 4 + lane // 32)
        i_of = row % 2 - (lane // 16) % 2 + 1
        for k in range(3):
            for l in range(4):
                block = jnp.zeros((32, 128), F32)
                if l < 3:
                    for i in range(3):
                        for j in range(3):
                            t = (i * 3 + j) * 3 + k
                            value = spread[8 * t + l : 8 * t + l + 1, :]
                            block = jnp.where((j_of == j) & (i_of == i), value, block)
                at = 128 * k + 32 * l
                w1[at : at + 32, 128 * tile : 128 * tile + 128] = block.astype(BF16)

    spread[0:216, :] = spread_rows(wl_ref, tmp)
    row = iota((16, 128), 0)
    lane = iota((16, 128), 1)
    i_of = (lane // 16) % 2 - row // 8 + 1
    for tile in range(2):
        q_of = tile * 4 + lane // 32
        j_of = jnp.where(q_of < STEP, q_of - row % 8 + 2, -1)
        for k in range(3):
            for l in range(3):
                block = jnp.zeros((16, 128), F32)
                for i in range(3):
                    for j in range(3):
                        t = (i * 3 + j) * 3 + k
                        value = spread[8 * t + l : 8 * t + l + 1, :]
                        block = jnp.where((j_of == j) & (i_of == i), value, block)
                at = 16 * (3 * k + l)
                w3[at : at + 16, 128 * tile : 128 * tile + 128] = block.astype(BF16)

    take = (iota((16, 128), 1) % 16 == iota((16, 128), 0)).astype(F32).astype(BF16)
    spread[...] = nn(wm_ref[...].reshape(81 * 16, 16), take)
    odd = (iota((16, 128), 1) // 16) % 2 == 1
    p_of = iota((16, 128), 1) // 32
    for k in range(3):
        for l in range(3):
            w2[3 * k + l, 192:256, :] = jnp.zeros((64, 256), BF16)
            for ra in range(2):
                values = []
                for j in range(3):
                    t0 = (((1 - ra) * 3 + j) * 3 + k) * 3 + l
                    t1 = (((2 - ra) * 3 + j) * 3 + k) * 3 + l
                    values.append(
                        jnp.where(odd, spread[16 * t1 : 16 * t1 + 16, :], spread[16 * t0 : 16 * t0 + 16, :])
                    )
                for q in range(STEP):
                    for tile in range(2):
                        block = jnp.zeros((16, 128), F32)
                        for j in range(3):
                            block = jnp.where(p_of == q + j - 4 * tile, values[j], block)
                        at = 32 * q + 16 * ra
                        w2[3 * k + l, at : at + 16, 128 * tile : 128 * tile + 128] = block.astype(BF16)


def shifted(values, by, edge):
    rows = values.shape[0]
    moved = pltpu.roll(values, by % rows, 0)
    return jnp.where(iota(values.shape, 0) % WB == edge, 0.0, moved)


def copy_matrix(e_ref):
    for m in range(BLOCKS):
        source = iota((256, 128), 0)
        lane = iota((256, 128), 1)
        shift, inner = lane // 32, lane % 32
        column, ref_row = 6 * m - 2 + inner // 2, inner % 2
        used = (inner < 20) & (column >= 0) & (column < WA) & (shift < 3)
        hit = used & (source == shift * NA + ref_row * WA + column)
        e_ref[:, 128 * m : 128 * m + 128] = jnp.where(hit, 1.0, 0.0).astype(BF16)


def unit_slices(values, unit, plane, rows):
    values = values.astype(F32)
    scale = lax.rsqrt(jnp.sum(values * values, axis=1, keepdims=True) + EPS_NORM)
    normed = values * scale
    mine = jnp.where(plane == 0, normed[:, 0:HALF], normed[:, HALF : 2 * HALF])
    for s in range(32):
        g, t = s // 4, s % 4
        at = 8 * s
        unit[at // rows, at % rows : at % rows + 8, :] = mine[8 * g : 8 * g + 8, 128 * t : 128 * t + 128].astype(BF16)


def squares_of(feats, out_ref):
    values = feats.astype(F32)
    sums = jnp.sum(values * values, axis=1, keepdims=True)
    for t in range(4):
        wide = jnp.broadcast_to(sums[128 * t : 128 * t + 128], (128, 128))
        out_ref[t : t + 1, :] = jnp.transpose(wide)[0:1, :]


def kernel(
    sizes, owner_hbm, valid_hbm, bf_hbm, bm_hbm, bl_hbm, q_hbm, t_hbm, wf_hbm, wm_hbm, wl_hbm,
    out_ref,
    owner_ref, valid_ref, bf_ref, bm_ref, bl_ref, q_ref, t_ref, wf_ref, wm_ref, wl_ref, unit, recv_a, cand, recv_b, piece, gath, sq_own, sq_oth, part, part_oth,
    tmp, spread, w1, w2, w3, e_ref, vbuf, xbuf, h1, h2, total, loads, sems,
):
    group, depth, inner, rows = sizes
    me = lax.axis_index("pair")
    plane = lax.axis_index("trow")
    z = lax.rem(me // inner, depth)
    g = (me // (inner * depth)) * inner + lax.rem(me, inner)

    def at(g_of, z_of):
        return ((g_of // inner) * depth + z_of) * inner + lax.rem(g_of, inner)

    cores, columns = min(2, inner), max(1, inner // 2)
    layers = group // inner
    core, x, layer = lax.rem(g, cores), lax.rem(g // cores, columns), g // inner
    steps = [(dy, dx, dc) for dy in range(layers) for dx in range(columns) for dc in range(cores)]
    steps = sorted(steps, key=lambda s: (-s[0] - min(s[1], columns - s[1]), -s[2]))[:-1]
    members = [
        (lax.rem(layer + dy, layers) * columns + lax.rem(x + dx, columns)) * cores + lax.rem(core + dc, cores)
        for dy, dx, dc in steps
    ]
    others = [
        lax.rem(z + o, depth) for o in sorted(range(1, depth), key=lambda o: -min(o, depth - o))
    ]

    barrier = pltpu.get_barrier_semaphore()

    def greet(pair, trow):
        pl.semaphore_signal(barrier, inc=1, device_id=(pair, trow), device_id_type=MESH)

    for other in others:
        greet(at(g, other), plane)
    for member in members:
        greet(at(member, z), plane)
    greet(me, 1 - plane)

    local = [
        pltpu.make_async_copy(src, dst, loads.at[i])
        for i, (src, dst) in enumerate(
            (
                (q_hbm.at[0], q_ref),
                (wf_hbm, wf_ref),
                (wl_hbm, wl_ref),
                (wm_hbm, wm_ref),
                (t_hbm.at[0], t_ref),
                (owner_hbm, owner_ref),
                (valid_hbm, valid_ref),
                (bf_hbm, bf_ref),
                (bm_hbm, bm_ref),
                (bl_hbm, bl_ref),
            )
        )
    ]
    for copy in local:
        copy.start()
    copy_matrix(e_ref)
    local[0].wait()
    unit_slices(q_ref[...], unit, plane, rows)
    for copy in local[1:4]:
        copy.wait()
    prepare(wf_ref, wm_ref, wl_ref, tmp, spread, w1, w2, w3)
    for copy in local[4:]:
        copy.wait()
    squares_of(t_ref[...], sq_own)

    pl.semaphore_wait(barrier, (depth - 1) + (group - 1) + 1)

    def send(src, dst, k, pair, trow):
        copy = pltpu.make_async_remote_copy(
            src_ref=src,
            dst_ref=dst,
            send_sem=sems.at[2 * k],
            recv_sem=sems.at[2 * k + 1],
            device_id=(pair, trow),
            device_id_type=MESH,
        )
        copy.start()
        return copy

    def wait(ref, k):
        pltpu.make_async_copy(ref, ref, sems.at[k]).wait()

    owner = owner_ref[0]
    owner_g = (owner // (inner * depth)) * inner + lax.rem(owner, inner)
    owner_z = lax.rem(owner // inner, depth)

    for member in members:
        send(unit.at[member], recv_a.at[g], 0, at(member, z), plane)
    squares = send(sq_own, sq_oth, 3, me, 1 - plane)
    recv_a[g] = unit[g]
    if group > 1:
        wait(recv_a.at[pl.ds(0, group - 1)], 1)
    chosen = recv_a[owner_g]
    cand[...] = chosen
    recv_b[z] = chosen

    for other in others:
        send(cand, recv_b.at[z], 1, at(g, other), plane)
    wait(recv_b.at[pl.ds(0, depth - 1)], 3)
    chosen = recv_b[owner_z]
    piece[...] = chosen
    gath[g] = chosen

    for member in members:
        send(piece, gath.at[g], 2, at(member, z), plane)
    if group > 1:
        wait(gath.at[pl.ds(0, group - 1)], 5)
    lines = []
    for line in range(8):
        tiles = []
        for t in range(4):
            first = 8 * (4 * line + t)
            tiles.append(gath[first // rows, first % rows : first % rows + 8, :].astype(F32))
        lines.append(jnp.concatenate(tiles, axis=1))
    window = jnp.concatenate(lines, axis=0).astype(BF16)

    blank = jnp.zeros((NA, HALF), BF16)
    partial = []
    for c in range(CHUNKS):
        first = c * (256 // CHUNKS)
        last = first + 256 // CHUNKS
        part[first:last] = nt(t_ref[first:last, :], jnp.concatenate([window, blank], axis=0)) + nt(
            t_ref[256 + first : 256 + last, :], jnp.concatenate([blank, window], axis=0)
        )
        partial.append(send(part.at[pl.ds(first, 256 // CHUNKS)], part_oth.at[pl.ds(first, 256 // CHUNKS)], 4 + c, me, 1 - plane))

    vbuf[0:WB, :] = jnp.zeros((WB, 128), F32)
    vbuf[WB + NB : 2 * WB + NB, :] = jnp.zeros((WB, 128), F32)
    b1 = bias_row(bf_ref, 256)
    b2 = bias_row(bm_ref, 32 * STEP)
    squares.wait()
    columns = []
    for t in range(4):
        both = sq_own[t : t + 1, :] + sq_oth[t : t + 1, :]
        columns.append(jnp.transpose(jnp.broadcast_to(both, (128, 128))))
    inverse = lax.rsqrt(jnp.concatenate(columns, axis=0) + EPS_NORM)
    live = iota((NB, 128), 0) // WB < valid_ref[0]

    for copy in partial:
        copy.wait()
    both = part[...] + part_oth[...]
    swapped = pltpu.roll(both, 64, 1)
    low = iota((256, 128), 1) < 64
    raw = jnp.concatenate([jnp.where(low, both, swapped), jnp.where(low, swapped, both)], axis=0)
    corr = jnp.where(live, math.sqrt(1024) * raw * inverse, 0.0)
    peak_target = jnp.max(jnp.abs(corr), axis=0, keepdims=True)
    vbuf[WB : WB + NB, :] = corr
    start = pl.multiple_of(plane * (6 * WB), 6 * WB)
    near = vbuf[pl.ds(start, 12 * WB), :]
    peak_query = jnp.max(jnp.abs(near), axis=1, keepdims=True)
    volume = near * (near * (1.0 / (peak_query + EPS_PEAK))) * (near * (1.0 / (peak_target + EPS_PEAK)))
    low = iota((12 * WB, 128), 1) < 64
    chosen = [jnp.where(low, shifted(volume, 1, 0), volume), shifted(volume, -1, WB - 1)]
    xbuf[...] = nn(jnp.concatenate(chosen, axis=1).astype(BF16), e_ref[...]).astype(BF16)

    pad = pl.multiple_of((1 - plane) * WB, WB)

    lane = iota((10 * WB, 256), 1)
    for m in range(BLOCKS):
        taps = [xbuf[WB * k : WB * k + 10 * WB, 128 * m : 128 * m + 128] for k in range(3)]
        acc = nn(jnp.concatenate(taps[0:2], axis=1), w1[0:256, :]) + nn(taps[2], w1[256:384, :])
        hidden = jnp.maximum(acc + b1, 0.0)
        if m == 0:
            hidden = jnp.where(lane < 32, 0.0, hidden)
        if m == BLOCKS - 1:
            hidden = jnp.where(lane >= 32 * (WA - 6 * m + 1), 0.0, hidden)
        zero = jnp.zeros((WB, 256), BF16)
        edge = pl.multiple_of(plane * (10 * WB), WB)
        for l in range(3):
            h1[m, l, pl.ds(edge, WB), :] = zero
        h1[m, 0, pl.ds(pad, 10 * WB), :] = shifted(hidden, 1, 0).astype(BF16)
        h1[m, 1, pl.ds(pad, 10 * WB), :] = hidden.astype(BF16)
        h1[m, 2, pl.ds(pad, 10 * WB), :] = shifted(hidden, -1, WB - 1).astype(BF16)

    edge = pl.multiple_of(plane * (9 * WB), WB)
    for m in range(BLOCKS):
        acc = jnp.zeros((9 * WB, 256), F32)
        for k in range(3):
            for l in range(3):
                acc = acc + nt(h1[m, l, WB * k : WB * k + 9 * WB, :], w2[3 * k + l])
        hidden = jnp.maximum(acc + b2, 0.0)
        if m == BLOCKS - 1:
            hidden = jnp.where(iota((9 * WB, 256), 1) < 32 * (WA - STEP * m), hidden, 0.0)
        h2[pl.ds(edge, WB), 256 * m : 256 * m + 256] = jnp.zeros((WB, 256), BF16)
        h2[pl.ds(pad, 9 * WB), 256 * m : 256 * m + 256] = hidden.astype(BF16)

    column = iota((16, 8 * WB), 1) % WB
    total[...] = jnp.zeros_like(total)
    for m in range(BLOCKS):
        acc = nt(w3[...], h2[:, 256 * m : 256 * m + 256])
        sums = []
        for l in range(3):
            terms = [acc[16 * (3 * k + l) : 16 * (3 * k + l) + 16] for k in range(3)]
            moved = [terms[0]] + [pltpu.roll(terms[k], 12 * WB - WB * k, 1) for k in (1, 2)]
            sums.append(moved[0][:, 0 : 8 * WB] + moved[1][:, 0 : 8 * WB] + moved[2][:, 0 : 8 * WB])
        block = sums[1]
        block = block + jnp.where(column == 0, 0.0, pltpu.roll(sums[0], 1, 1))
        block = block + jnp.where(column == WB - 1, 0.0, pltpu.roll(sums[2], 8 * WB - 1, 1))
        for ra in range(2):
            total[ra, STEP * m : STEP * m + 8, :] += block[8 * ra : 8 * ra + 8]
    row = plane * 8 + iota((WA, 8 * WB), 1) // WB
    for ra in range(2):
        result = total[ra, 1 : 1 + WA, :] + bl_ref[0]
        out_ref[0, WA * ra : WA * ra + WA, :] = jnp.where(row < valid_ref[0], result, 0.0)

    if group > 1:
        wait(recv_a.at[pl.ds(0, group - 1)], 0)
        wait(gath.at[pl.ds(0, group - 1)], 4)
    wait(recv_b.at[pl.ds(0, depth - 1)], 2)


def layout_of(n):
    inner = min(8, max(1, n // 2))
    depth = min(8, n // inner)
    group = n // depth
    return group, depth, inner, 256 // group


def score(owner, valid, b_first, b_middle, b_last, bank, feats, wf, wm, wl, n):
    hbm = pl.BlockSpec(memory_space=pltpu.HBM)
    sizes = layout_of(n)
    group, depth, _, rows = sizes
    return pl.pallas_call(
        functools.partial(kernel, sizes),
        out_shape=pltpu.VMEM((1, NA, 8 * WB), F32),
        in_specs=[hbm] * 10,
        out_specs=pl.BlockSpec(memory_space=pltpu.VMEM),
        scratch_shapes=[
            pltpu.SMEM((1,), jnp.int32),
            pltpu.SMEM((1,), jnp.int32),
            pltpu.SMEM((16,), F32),
            pltpu.SMEM((16,), F32),
            pltpu.SMEM((1,), F32),
            pltpu.VMEM((NA, 2 * HALF), BF16),
            pltpu.VMEM((NB, HALF), BF16),
            pltpu.VMEM((27, 3, 16), BF16),
            pltpu.VMEM((81, 16, 16), BF16),
            pltpu.VMEM((27, 3, 16), BF16),
            pltpu.VMEM((group, rows, 128), BF16),
            pltpu.VMEM((group, rows, 128), BF16),
            pltpu.VMEM((rows, 128), BF16),
            pltpu.VMEM((depth, rows, 128), BF16),
            pltpu.VMEM((rows, 128), BF16),
            pltpu.VMEM((group, rows, 128), BF16),
            pltpu.VMEM((8, 128), F32),
            pltpu.VMEM((8, 128), F32),
            pltpu.VMEM((256, 128), F32),
            pltpu.VMEM((256, 128), F32),
            pltpu.VMEM((27, 8, 128), F32),
            pltpu.VMEM((81 * 16, 128), F32),
            pltpu.VMEM((384, 256), BF16),
            pltpu.VMEM((9, 256, 256), BF16),
            pltpu.VMEM((144, 256), BF16),
            pltpu.VMEM((256, 768), BF16),
            pltpu.VMEM((NB + 2 * WB, 128), F32),
            pltpu.VMEM((12 * WB, 768), BF16),
            pltpu.VMEM((BLOCKS, 3, 11 * WB, 256), BF16),
            pltpu.VMEM((12 * WB, 1536), BF16),
            pltpu.VMEM((2, 40, 8 * WB), F32),
            pltpu.SemaphoreType.DMA((10,)),
            pltpu.SemaphoreType.DMA((8 + 2 * CHUNKS,)),
        ],
        compiler_params=pltpu.CompilerParams(
            collective_id=0, has_side_effects=True, vmem_limit_bytes=60 * 1024 * 1024
        ),
        name="pair_scores",
    )(owner, valid, b_first, b_middle, b_last, bank, feats, wf, wm, wl)


def per_device(
    query_bank, ref_owner, target_feat, valid_rows, w_first, b_first, w_middle, b_middle, w_last, b_last
):
    wf = jnp.transpose(w_first, (1, 2, 3, 4, 5, 0)).reshape(27, 3, 16)
    wl = jnp.transpose(w_last, (0, 2, 3, 4, 5, 1)).reshape(27, 3, 16)
    wm = jnp.transpose(w_middle, (2, 3, 4, 5, 0, 1)).reshape(81, 16, 16)
    n = lax.axis_size("pair")
    return score(ref_owner, valid_rows, b_first, b_middle, b_last, query_bank, target_feat, wf, wm, wl, n)


def solution(mesh):
    in_specs = (
        P("pair", None, None),
        P(),
        P("pair", None, "trow"),
        P("pair"),
        P(),
        P(),
        P(),
        P(),
        P(),
        P(),
    )
    out_specs = P("pair", None, "trow")
    return jax.shard_map(
        per_device, mesh=mesh, in_specs=in_specs, out_specs=out_specs, check_vma=False
    )
```
